32 devices in a mesh: freq: 8 (over y, x, core), rcv: 4 (over z).
Axes of the slice: x: 2, y: 2, z: 4, core: 2. Of those that a mesh axis runs over, the one named last changes fastest.
Arguments:
- green_freq: float32 [2, 8, 2304, 2304], P(None, 'freq', 'rcv'), may hold values from -6 to 6
- data_matrix: float32 [2, 8, 2304, 2304], P(None, 'freq', 'rcv'), may hold values from -0.09375 to 0.09375
- shot_panels: float32 [2, 8, 2304, 256], P(None, 'freq', 'rcv'), may hold values from -6 to 6
- wavelet: float32 [2, 8], P(None, 'freq'), may hold values from -1.5 to 1.5
- sources: int32 [256], replicated, may hold values from 0 to 2303, as said below
- support: int32 [8, 2304], replicated, may hold values 0 or 1
- threshold: float32 [1], replicated, may hold values from 3 to 7
Outputs:
- green_next: float32 [2, 8, 2304, 2304], P(None, 'freq', 'rcv')
- residual: float32 [2, 8, 2304, 256], P(None, 'freq', 'rcv')
The draws below stay inside these ranges and needn't reach their ends.
Inputs may be any that keep to these rules, and one draw needn't show every extreme that they name: `sources`: 256 distinct source positions. `support`: a 0/1 mask over time samples and source positions.
All inputs are finite; a program needn't handle non-finite values.
Results may differ from the reference program's by a relative error of at most 0.00013.
Values sent between devices are 32-bit elements; how exact they have to be, the bound alone decides.
A program may use at most 128 MiB of HBM per device.

```python
import math
import jax
import jax.numpy as jnp
from jax import lax

NGRID = 2304
NC = 256
NF = 8


def draw_sources(key, part):
    order = jax.random.permutation(jax.random.fold_in(key, 11), NGRID)
    return order[:NC].astype(jnp.int32)


def place_ends(entries, stream_key, smallest, high):
    place = [jax.random.randint(jax.random.fold_in(stream_key, axis), (), 0, length) for axis, length in enumerate(entries.shape)]
    longest = entries.shape.index(max(entries.shape))
    neighbour = place[:longest] + [(place[longest] + 1) % entries.shape[longest]] + place[longest + 1:]
    return entries.at[tuple(place)].set(smallest).at[tuple(neighbour)].set(high)


def steps_of(rng, shape, pieces, least, largest):
    gain = 1.0
    for position, parts in pieces:
        steps = jax.random.uniform(jax.random.fold_in(jax.random.fold_in(rng, 6), position), (parts,), jnp.float32, least / len(pieces), largest / len(pieces))
        gain = gain * jnp.repeat(jnp.exp(steps), shape[position] // parts).reshape((-1,) + (1,) * (len(shape) - 1 - position))
    return gain


def normal_values(key, shape, width, most, cuts=(), kind=jnp.bfloat16):
    array = jax.random.normal(key, shape, jnp.float32) * width
    if len(cuts) > 0:
        array = steps_of(key, shape, cuts, -0.22, 0.18) * array
    return jnp.clip(array, min=-most, max=most).astype(kind)


def setup_inputs(seed: int = 0) -> dict:
    key_list = jax.random.split(jax.random.key(seed), 8)
    green_freq = normal_values(key_list[0], (2, NF, NGRID, NGRID), 1.0, 6.0, ((1, 8), (2, 4)), jnp.float32)
    data_matrix = normal_values(key_list[1], (2, NF, NGRID, NGRID), (2 * NGRID) ** -0.5, 0.09375, ((1, 8), (2, 4)), jnp.float32)
    shot_panels = normal_values(key_list[2], (2, NF, NGRID, NC), 1.0, 6.0, ((1, 8), (2, 4)), jnp.float32)
    wavelet = jnp.clip(jax.random.uniform(key_list[3], (2, NF), jnp.float32, -1.5, 1.5) * steps_of(key_list[3], (2, NF), ((1, 8),), -0.4, 0.0), -1.5, 1.5)
    sources = draw_sources(jax.random.fold_in(key_list[7], 71), 0)
    support = place_ends((jax.random.randint(key_list[5], (NF, NGRID), 0, 4) < 3).astype(jnp.int32), jax.random.fold_in(key_list[5], 1), 0, 1)
    threshold = jnp.clip(jax.random.uniform(key_list[6], (1,), jnp.float32, 3.0, 7.0), 3.0, 7.0)
    return {"green_freq": green_freq, "data_matrix": data_matrix, "shot_panels": shot_panels, "wavelet": wavelet, "sources": sources, "support": support, "threshold": threshold}


HIGHEST = lax.Precision.HIGHEST

def complex_product(left_pair, right_pair, pattern):
    left_real, left_imag = left_pair
    right_real, right_imag = right_pair
    real_part = jnp.einsum(pattern, left_real, right_real, precision=HIGHEST) - jnp.einsum(pattern, left_imag, right_imag, precision=HIGHEST)
    imag_part = jnp.einsum(pattern, left_real, right_imag, precision=HIGHEST) + jnp.einsum(pattern, left_imag, right_real, precision=HIGHEST)
    return (real_part, imag_part)

def conj_product(left_pair, right_pair, pattern):
    left_real, left_imag = left_pair
    right_real, right_imag = right_pair
    real_part = jnp.einsum(pattern, left_real, right_real, precision=HIGHEST) + jnp.einsum(pattern, left_imag, right_imag, precision=HIGHEST)
    imag_part = jnp.einsum(pattern, left_real, right_imag, precision=HIGHEST) - jnp.einsum(pattern, left_imag, right_real, precision=HIGHEST)
    return (real_part, imag_part)

def shrink_spectra(spectra, keep, shrink_level):
    n_freq = spectra.shape[1]
    grid = jnp.arange(n_freq, dtype=jnp.int32)
    phase = grid[:, None] * grid[None, :] % n_freq
    angle = phase.astype(jnp.float32) * (2.0 * math.pi / n_freq)
    cos_table = jnp.cos(angle)
    sin_table = jnp.sin(angle)
    pattern = 'tf,f...->t...'
    time_real = jnp.einsum(pattern, cos_table, spectra[0], precision=HIGHEST) - jnp.einsum(pattern, sin_table, spectra[1], precision=HIGHEST)
    time_imag = jnp.einsum(pattern, sin_table, spectra[0], precision=HIGHEST) + jnp.einsum(pattern, cos_table, spectra[1], precision=HIGHEST)
    magnitude = jnp.sqrt(time_real * time_real + time_imag * time_imag)
    factor = jnp.maximum(magnitude - shrink_level, 0.0) / jnp.maximum(magnitude, shrink_level) * keep
    kept_real = factor * time_real
    kept_imag = factor * time_imag
    back_real = (jnp.einsum(pattern, cos_table, kept_real, precision=HIGHEST) + jnp.einsum(pattern, sin_table, kept_imag, precision=HIGHEST)) / n_freq
    back_imag = (jnp.einsum(pattern, cos_table, kept_imag, precision=HIGHEST) - jnp.einsum(pattern, sin_table, kept_real, precision=HIGHEST)) / n_freq
    return jnp.stack([back_real, back_imag])

def reference(green_freq, data_matrix, shot_panels, wavelet, sources, support, threshold):
    picked = jnp.take(green_freq, sources, axis=3)

    def per_frequency(inputs):
        green_cols, data_now, shots_now, wave_now = inputs
        wave_real = wave_now[0]
        wave_imag = wave_now[1]
        data_pair = (data_now[0], data_now[1])
        multiple = complex_product(data_pair, (green_cols[0], green_cols[1]), 'rk,kc->rc')
        resid_real = shots_now[0] - (wave_real * green_cols[0] - wave_imag * green_cols[1] - multiple[0])
        resid_imag = shots_now[1] - (wave_real * green_cols[1] + wave_imag * green_cols[0] - multiple[1])
        adjoint = conj_product(data_pair, (resid_real, resid_imag), 'rk,rc->kc')
        dir_real = wave_real * resid_real + wave_imag * resid_imag - adjoint[0]
        dir_imag = wave_real * resid_imag - wave_imag * resid_real - adjoint[1]
        pushed = complex_product(data_pair, (dir_real, dir_imag), 'rk,kc->rc')
        image_real = wave_real * dir_real - wave_imag * dir_imag - pushed[0]
        image_imag = wave_real * dir_imag + wave_imag * dir_real - pushed[1]
        norm_dir = jnp.sum(dir_real * dir_real + dir_imag * dir_imag)
        norm_img = jnp.sum(image_real * image_real + image_imag * image_imag)
        return (jnp.stack([resid_real, resid_imag]), jnp.stack([dir_real, dir_imag]), norm_dir, norm_img)
    mapped = lax.map(per_frequency, (jnp.moveaxis(picked, 1, 0), jnp.moveaxis(data_matrix, 1, 0), jnp.moveaxis(shot_panels, 1, 0), jnp.moveaxis(wavelet, 1, 0)))
    residual = jnp.moveaxis(mapped[0], 0, 1)
    direction = jnp.moveaxis(mapped[1], 0, 1)
    step_size = jnp.sum(mapped[2]) / jnp.sum(mapped[3])
    updated = green_freq.at[:, :, :, sources].add(step_size * direction)
    rows_first = jnp.moveaxis(updated, 2, 0)
    keep = support.astype(jnp.float32)

    def shrink_row(spectra_row):
        return shrink_spectra(spectra_row, keep, threshold[0])
    shrunk = lax.map(shrink_row, rows_first)
    green_next = jnp.moveaxis(shrunk, 0, 2)
    return (green_next, residual)
```

```python
import functools
import math

import jax
import jax.numpy as jnp
from jax import lax
from jax.experimental import pallas as pl
from jax.experimental.pallas import tpu as pltpu
from jax.sharding import PartitionSpec as P

HIGH = lax.Precision.HIGH
MESH = pl.DeviceIdType.MESH


def transform(points, sign):
    count = len(points)
    if count == 1:
        return points
    if count % 2:
        out = []
        for t in range(count):
            real, imag = points[0]
            for f in range(1, count):
                angle = sign * 2.0 * math.pi * (f * t % count) / count
                c, s = math.cos(angle), math.sin(angle)
                real = real + (c * points[f][0] - s * points[f][1])
                imag = imag + (s * points[f][0] + c * points[f][1])
            out.append((real, imag))
        return out
    even = transform(points[0::2], sign)
    odd = transform(points[1::2], sign)
    low, high = [], []
    for k in range(count // 2):
        er, ei = even[k]
        r, i = odd[k]
        angle = 8 * k / count
        if k == 0:
            tr, ti = r, i
        elif angle == 2:
            tr, ti = (-i, r) if sign > 0 else (i, -r)
        elif angle == 1:
            h = math.sqrt(0.5)
            tr, ti = (h * (r - i), h * (r + i)) if sign > 0 else (h * (r + i), h * (i - r))
        elif angle == 3:
            h = math.sqrt(0.5)
            tr, ti = (-h * (r + i), h * (r - i)) if sign > 0 else (h * (i - r), -h * (r + i))
        else:
            c = math.cos(2 * math.pi * k / count)
            s = sign * math.sin(2 * math.pi * k / count)
            tr, ti = c * r - s * i, s * r + c * i
        low.append((er + tr, ei + ti))
        high.append((er - tr, ei - ti))
    return low + high


def shrink_points(points, keep, level):
    count = len(points)
    timed = transform(points, 1)
    kept = []
    for t, (real, imag) in enumerate(timed):
        size = jnp.sqrt(real * real + imag * imag)
        factor = jnp.maximum(size - level, 0.0) / jnp.maximum(size, level) * keep[t : t + 1]
        factor = factor * (1.0 / count)
        kept.append((factor * real, factor * imag))
    return transform(kept, -1)


def shrink_body(scal_ref, keep_ref, *refs):
    *x_refs, o_ref = refs
    x_ref = x_refs[0]
    count = x_ref.shape[1]
    level = scal_ref[0]

    def lanes(j, carry):
        at = pl.ds(pl.multiple_of(j * 128, 128), 128)
        points = [(x_ref[0, f, :, at], x_ref[1, f, :, at]) for f in range(count)]
        if len(x_refs) == 2:
            d_ref = x_refs[1]
            step = scal_ref[1]
            points = [
                (r + step * d_ref[0, f, :, at], i + step * d_ref[1, f, :, at])
                for f, (r, i) in enumerate(points)
            ]
        out = shrink_points(points, keep_ref[:, at], level)
        for f in range(count):
            o_ref[0, f, :, at] = out[f][0]
            o_ref[1, f, :, at] = out[f][1]
        return carry

    lax.fori_loop(0, x_ref.shape[3] // 128, lanes, 0)


def shrink_call(scalars, keep, arrays):
    two, count, rows, width = arrays[0].shape
    tile = 8 if rows % 8 == 0 else rows
    if rows % 24 == 0 and width <= 512:
        tile = 24
    block = pl.BlockSpec((two, count, tile, width), lambda j: (0, 0, j, 0))
    size = arrays[0].size * 4
    return pl.pallas_call(
        shrink_body,
        grid=(rows // tile,),
        in_specs=[
            pl.BlockSpec(memory_space=pltpu.SMEM),
            pl.BlockSpec((count, width), lambda j: (0, 0)),
        ]
        + [block] * len(arrays),
        out_specs=block,
        out_shape=jax.ShapeDtypeStruct(arrays[0].shape, jnp.float32),
        cost_estimate=pl.CostEstimate(
            flops=40 * arrays[0].size, bytes_accessed=size * (1 + len(arrays)), transcendentals=0
        ),
    )(scalars, keep, *arrays)


def merge_body(mask_ref, hot_ref, cols_ref, back_ref, o_ref):
    hot = hot_ref[...]
    mask = mask_ref[...] > 0.5
    for part in range(2):
        x = cols_ref[:, part * hot.shape[0] : (part + 1) * hot.shape[0]]
        hi = x.astype(jnp.bfloat16)
        rest = x - hi.astype(jnp.float32)
        mid = rest.astype(jnp.bfloat16)
        low = (rest - mid.astype(jnp.float32)).astype(jnp.bfloat16)
        spread = (
            jnp.dot(hi, hot, preferred_element_type=jnp.float32)
            + jnp.dot(mid, hot, preferred_element_type=jnp.float32)
        ) + jnp.dot(low, hot, preferred_element_type=jnp.float32)
        o_ref[part, 0] = jnp.where(mask, spread, back_ref[part, 0])


def merge_call(mask, hot, cols, back):
    two, one, rows, width = back.shape
    picked = hot.shape[0]
    tile = rows // 4 if rows % 32 == 0 else rows
    return pl.pallas_call(
        merge_body,
        grid=(rows // tile,),
        in_specs=[
            pl.BlockSpec((1, width), lambda i: (0, 0)),
            pl.BlockSpec((picked, width), lambda i: (0, 0)),
            pl.BlockSpec((tile, two * picked), lambda i: (i, 0)),
            pl.BlockSpec((two, one, tile, width), lambda i: (0, 0, i, 0)),
        ],
        out_specs=pl.BlockSpec((two, one, tile, width), lambda i: (0, 0, i, 0)),
        out_shape=jax.ShapeDtypeStruct(back.shape, jnp.float32),
    )(mask, hot, cols, back)


def dots(lhs, rhs, contract):
    return lax.dot_general(lhs, rhs, (contract, ((), ())), precision=HIGH)


def apply_rows(data_real, data_imag, both, flipped):
    ahead = (((1,), (0,)))
    return dots(data_real, both, ahead) + dots(data_imag, flipped, ahead)


ANY = pl.BlockSpec(memory_space=pltpu.HBM)
VMEM = pl.BlockSpec(memory_space=pltpu.VMEM)
DMA = pltpu.SemaphoreType.DMA


SMEM = pl.BlockSpec(memory_space=pltpu.SMEM)


def halves(x):
    hi = x.astype(jnp.bfloat16)
    return hi, (x - hi.astype(jnp.float32)).astype(jnp.bfloat16)


def thirds(x):
    hi, mid = halves(x)
    rest = x - hi.astype(jnp.float32) - mid.astype(jnp.float32)
    return jnp.concatenate([hi, mid, rest.astype(jnp.bfloat16)], axis=0)


def select(x, hot):
    rows = x.shape[0]
    out = jnp.dot(thirds(x), hot, preferred_element_type=jnp.float32)
    return (out[:rows] + out[rows : 2 * rows]) + out[2 * rows :]


def six(parts, contract):
    total = None
    for (lh, ll), (rh, rl) in parts:
        for x, y in ((lh, rl), (ll, rh), (lh, rh)):
            term = lax.dot_general(
                x, y, (contract, ((), ())), preferred_element_type=jnp.float32
            )
            total = term if total is None else total + term
    return total


def piece_of(width):
    for piece in (768, 512, 256):
        if width % piece == 0:
            return piece
    return width


def apply_data(data, x_ref, acc):
    half = x_ref.shape[1] // 2
    piece = piece_of(x_ref.shape[0])
    acc[...] = jnp.zeros_like(acc)

    def chunk(i, carry):
        at = pl.ds(pl.multiple_of(i * piece, piece), piece)
        x = x_ref[at, :]
        turned = jnp.concatenate([-x[:, half:], x[:, :half]], axis=1)
        acc[...] += six(
            [
                ((data[0, 0, :, at], data[0, 1, :, at]), halves(x)),
                ((data[1, 0, :, at], data[1, 1, :, at]), halves(turned)),
            ],
            ((1,), (0,)),
        )
        return carry

    lax.fori_loop(0, x_ref.shape[0] // piece, chunk, 0)


def apply_adjoint(data, x, out):
    half = x.shape[1] // 2
    piece = piece_of(out.shape[0])
    straight = halves(x)
    turned = halves(jnp.concatenate([x[:, half:], -x[:, :half]], axis=1))

    def chunk(i, carry):
        at = pl.ds(pl.multiple_of(i * piece, piece), piece)
        out[at, :] = six(
            [
                ((data[0, 0, :, at], data[0, 1, :, at]), straight),
                ((data[1, 0, :, at], data[1, 1, :, at]), turned),
            ],
            ((0,), (0,)),
        )
        return carry

    lax.fori_loop(0, out.shape[0] // piece, chunk, 0)


class Gather:
    def __init__(self, size, buf, sends, recvs):
        self.size, self.buf, self.sends, self.recvs = size, buf, sends, recvs
        self.z = lax.axis_index("rcv")

    def ways(self, step):
        z, last = self.z, self.size - 1
        rows = self.buf.shape[0] // self.size
        for way in range(2):
            if way == 0:
                block, to = jnp.maximum(z - step, 0), jnp.minimum(z + 1, last)
                sent = (z < last) & (z >= step)
                got = z >= step + 1
            else:
                block, to = jnp.minimum(z + step, last), jnp.maximum(z - 1, 0)
                sent = (z > 0) & (z + step <= last)
                got = z + 1 + step <= last
            part = self.buf.at[pl.ds(pl.multiple_of(block * rows, 8), rows), :]
            copy = pltpu.make_async_remote_copy(
                part, part, self.sends.at[way, step], self.recvs.at[way, step],
                device_id={"rcv": to}, device_id_type=MESH,
            )
            yield copy, sent, got

    def start(self, step):
        for copy, sent, _ in self.ways(step):
            pl.when(sent)(copy.start)

    def recv(self, step):
        for copy, _, got in self.ways(step):
            pl.when(got)(copy.wait_recv)

    def drain(self):
        for step in range(self.size - 1):
            for copy, sent, _ in self.ways(step):
                pl.when(sent)(copy.wait_send)


class Scatter:
    def __init__(self, size, terms, held, sends, recvs):
        self.size, self.terms, self.held = size, terms, held
        self.sends, self.recvs = sends, recvs
        self.z = lax.axis_index("rcv")

    def ways(self, step):
        z, last = self.z, self.size - 1
        rows = self.terms.shape[0] // self.size
        for way in range(2):
            if way == 0:
                far, to = z, jnp.minimum(z + 1, last)
                block = jnp.minimum(last - step + z, last)
                more, less = z < last, z > 0
            else:
                far, to = last - z, jnp.maximum(z - 1, 0)
                block = jnp.maximum(step - last + z, 0)
                more, less = z > 0, z < last
            own = self.terms.at[pl.ds(pl.multiple_of(block * rows, 8), rows), :]
            got = less & (step >= far - 1)
            yield way, own, to, more & (far == 0), more & (far > 0) & (step >= far), got

    def copy(self, src, way, step, to):
        return pltpu.make_async_remote_copy(
            src, self.held.at[way, step], self.sends.at[way, step], self.recvs.at[way, step],
            device_id={"rcv": to}, device_id_type=MESH,
        )

    def start(self, step):
        for way, own, to, first, later, _ in self.ways(step):
            pl.when(first)(self.copy(own, way, step, to).start)
            if step:
                self.pass_on(way, own, to, step, later)

    def pass_on(self, way, own, to, step, later):
        @pl.when(later)
        def _():
            self.held[way, step - 1] = self.held[way, step - 1] + own[...]
            self.copy(self.held.at[way, step - 1], way, step, to).start()

    def recv(self, step):
        for way, own, to, _, _, got in self.ways(step):
            pl.when(got)(self.copy(own, way, step, to).wait_recv)

    def drain(self):
        for step in range(self.size - 1):
            for way, own, to, first, later, _ in self.ways(step):
                pl.when(first | later)(self.copy(own, way, step, to).wait_send)


def greet(freqs, size):
    me = lax.axis_index("freq")
    z = lax.axis_index("rcv")
    barrier = pltpu.get_barrier_semaphore()
    for k in range(1, freqs):
        pl.semaphore_signal(
            barrier, inc=1, device_id={"freq": (me + k) % freqs}, device_id_type=MESH
        )
    for k in range(1, size):
        pl.semaphore_signal(barrier, inc=1, device_id={"rcv": (z + k) % size}, device_id_type=MESH)
    pl.semaphore_wait(barrier, freqs + size - 2)


LINE = 8


def rows_at(at, count):
    return pl.ds(pl.multiple_of(at, 8), count)


def main_body(
    freqs, size, level_ref, wave, srcs, support, green, data_hbm, shots_hbm,
    gathered, shrunk, back, cols_out, residual, hot_out, mask_out,
    big, data, whole, dir_all, adjoint, held, local, shots, image, hot, keep, keep_cols,
    pick_timed, dir_timed, cols, norms, freq_box, rcv_box,
    gload, sload, load, fsend, frecv, fown, bsend, brecv, bown,
    zsend, zrecv, dsend, drecv, down, csend, crecv, cown, nfs, nfr, nzs, nzr,
):
    me = lax.axis_index("freq")
    z = lax.axis_index("rcv")
    _, _, rows, width = green.shape
    deep = rows // freqs
    lines = deep // LINE
    picks = srcs.shape[1]
    half = picks // 2
    mine = rows_at(z * rows, rows)
    parts = gload.shape[0]
    tall = rows // parts

    def loading(j):
        at = rows_at(j * tall, tall)
        return pltpu.make_async_copy(green.at[:, 0, at, :], big.at[:, at, :], gload.at[j])

    for j in range(parts):
        loading(j).start()
    fetch_shots = pltpu.make_async_copy(shots_hbm.at[:, 0], shots, sload)
    fetch_shots.start()
    greet(freqs, size)

    def forth(i, k):
        to = (me + k) % freqs
        return pltpu.make_async_remote_copy(
            green.at[:, 0, rows_at(to * deep + i * LINE, LINE), :],
            gathered.at[:, me, pl.ds(i * LINE, LINE), :],
            fsend.at[i, k], frecv.at[i, k],
            device_id={"freq": to}, device_id_type=MESH,
        )

    for i in range(lines):
        for k in range(1, freqs):
            forth(i, k).start()

    place = lax.broadcasted_iota(jnp.int32, (width, picks), 0)
    hot_f32 = jnp.where(place == srcs[...], 1.0, 0.0)
    hot[...] = hot_f32.astype(jnp.bfloat16)

    def pick(j, carry):
        at = rows_at(j * tall, tall)
        loading(j).wait()
        for part in range(2):
            out = select(big[part, at, :], hot[...])
            to = rows_at(z * rows + j * tall, tall)
            for c in range(2):
                whole[c, to, part * half : (part + 1) * half] = out[:, c * half : (c + 1) * half]
        return carry

    lax.fori_loop(0, parts, pick, 0)
    first = [Gather(size, whole.at[c], zsend.at[c], zrecv.at[c]) for c in range(2)]
    second = [Gather(size, dir_all.at[c], zsend.at[2 + c], zrecv.at[2 + c]) for c in range(2)]
    sums = [
        Scatter(size, adjoint.at[c], held.at[c], zsend.at[4 + c], zrecv.at[4 + c])
        for c in range(2)
    ]
    last = size - 2
    first[0].start(0)
    own_part = pltpu.make_async_copy(
        big.at[:, rows_at(me * deep, deep), :], gathered.at[:, me], fown
    )
    own_part.start()
    keep[...] = support[...].astype(jnp.float32)
    keep_cols[...] = jnp.dot(
        keep[...].astype(jnp.bfloat16), hot[...], preferred_element_type=jnp.float32
    )
    for at in range(0, width, picks):
        hot_out[:, at : at + picks] = hot[at : at + picks, :].astype(jnp.float32).T.astype(
            jnp.bfloat16
        )
    mask_out[...] = jnp.dot(
        jnp.ones((8, picks), jnp.bfloat16), hot_out[...], preferred_element_type=jnp.float32
    )
    own_part.wait()
    fetch = pltpu.make_async_copy(data_hbm.at[:, 0], big, load)
    fetch.start()

    def split(j, carry):
        at = rows_at(j * 32, 32)
        for part in range(2):
            hi, lo = halves(big[part, at, :])
            data[part, 0, at, :] = hi
            data[part, 1, at, :] = lo
        return carry

    def shrink(lo, count):
        for i in range(lo, lo + count):
            for k in range(1, freqs):
                forth(i, k).wait_recv()
        block = pl.BlockSpec((2, freqs, LINE, width), lambda j: (0, 0, lo + j, 0))

        def body(ids, x_ref, o_ref):
            flat = x_ref[...].reshape(2 * freqs * LINE, width)
            got = select(flat, hot[...])
            at = rows_at((lo + ids.index[0]) * LINE, LINE)
            for part in range(2):
                for f in range(freqs):
                    row = (part * freqs + f) * LINE
                    pick_timed[f, at, part * picks : (part + 1) * picks] = got[row : row + LINE, :]
            shrink_body(level_ref, keep, x_ref, o_ref)

        pltpu.emit_pipeline(
            body, grid=(count,), in_specs=[block], out_specs=[block], _explicit_indices=True
        )(gathered, shrunk)

    def back_copy(i, k):
        to = (me + k) % freqs
        return pltpu.make_async_remote_copy(
            shrunk.at[:, to, pl.ds(i * LINE, LINE), :],
            back.at[:, 0, rows_at(me * deep + i * LINE, LINE), :],
            bsend.at[i, k], brecv.at[i, k],
            device_id={"freq": to}, device_id_type=MESH,
        )

    def back_own(i):
        return pltpu.make_async_copy(
            shrunk.at[:, me, pl.ds(i * LINE, LINE), :],
            back.at[:, 0, rows_at(me * deep + i * LINE, LINE), :],
            bown.at[i],
        )

    def give(lo, count):
        for i in range(lo, lo + count):
            for k in range(1, freqs):
                back_copy(i, k).start()
            back_own(i).start()

    def rows_copy(c, k):
        to = (me + k) % freqs
        return pltpu.make_async_remote_copy(
            dir_all.at[c, rows_at(z * rows + to * deep, deep), :], dir_timed.at[c, me],
            dsend.at[c, k], drecv.at[c, k],
            device_id={"freq": to}, device_id_type=MESH,
        )

    def rows_own(c):
        return pltpu.make_async_copy(
            dir_all.at[c, rows_at(z * rows + me * deep, deep), :], dir_timed.at[c, me], down.at[c]
        )

    wr, wi = wave[0], wave[1]
    re, im = slice(0, half), slice(half, 2 * half)

    def residual_of(c):
        apply_data(data, whole.at[c], image)
        at = slice(c * half, (c + 1) * half)
        pr, pi = whole[c, mine, re], whole[c, mine, im]
        rr = shots[0, :, at] - (wr * pr - wi * pi - image[:, re])
        ri = shots[1, :, at] - (wr * pi + wi * pr - image[:, im])
        residual[0, 0, :, at] = rr
        residual[1, 0, :, at] = ri
        local[c, :, re] = wr * rr + wi * ri
        local[c, :, im] = wr * ri - wi * rr
        apply_adjoint(data, jnp.concatenate([rr, ri], axis=1), adjoint.at[c])

    def direction_of(c):
        dir_all[c, mine, :] = local[c] - adjoint[c, mine, :]

        @pl.when(z > 0)
        def _():
            dir_all[c, mine, :] = dir_all[c, mine, :] - held[c, 0, last]

        @pl.when(z < size - 1)
        def _():
            dir_all[c, mine, :] = dir_all[c, mine, :] - held[c, 1, last]

    def send_direction(c):
        for k in range(1, freqs):
            rows_copy(c, k).start()
        rows_own(c).start()

    def image_of(c):
        apply_data(data, dir_all.at[c], image)
        dr, di = dir_all[c, mine, re], dir_all[c, mine, im]
        gr = wr * dr - wi * di - image[:, re]
        gi = wr * di + wi * dr - image[:, im]
        return jnp.sum(dr * dr + di * di), jnp.sum(gr * gr + gi * gi)

    first[0].recv(0)
    first[0].start(1)
    fetch.wait()
    lax.fori_loop(0, rows // 32, split, 0)
    fetch_shots.wait()
    first[0].recv(1)
    first[0].start(2)
    first[1].start(0)
    shrink(0, 2)
    first[0].recv(2)
    residual_of(0)
    sums[0].start(0)
    first[1].recv(0)
    first[1].start(1)
    shrink(2, 2)
    sums[0].recv(0)
    sums[0].start(1)
    first[1].recv(1)
    first[1].start(2)
    shrink(4, 1)
    sums[0].recv(1)
    sums[0].start(2)
    first[1].recv(2)
    residual_of(1)
    sums[1].start(0)
    sums[0].recv(2)
    direction_of(0)
    second[0].start(0)
    send_direction(0)
    shrink(5, 2)
    give(0, 2)
    sums[1].recv(0)
    sums[1].start(1)
    second[0].recv(0)
    second[0].start(1)
    shrink(7, 1)
    give(2, 1)
    sums[1].recv(1)
    sums[1].start(2)
    second[0].recv(1)
    second[0].start(2)
    shrink(8, lines - 8)
    give(3, 1)
    sums[1].recv(2)
    direction_of(1)
    second[1].start(0)
    send_direction(1)
    second[0].recv(2)
    ones = image_of(0)
    give(4, 1)
    second[1].recv(0)
    second[1].start(1)
    give(5, 1)
    second[1].recv(1)
    second[1].start(2)
    give(6, 1)
    second[1].recv(2)
    twos = image_of(1)

    for n in range(2):
        norms[n] = jnp.full((8, 128), ones[n] + twos[n])

    def spread(k):
        return pltpu.make_async_remote_copy(
            norms, freq_box.at[k], nfs.at[k], nfr.at[k],
            device_id={"freq": (me + k) % freqs}, device_id_type=MESH,
        )

    def across(k):
        return pltpu.make_async_remote_copy(
            rcv_box.at[0], rcv_box.at[k], nzs.at[k], nzr.at[k],
            device_id={"rcv": (z + k) % size}, device_id_type=MESH,
        )

    for k in range(1, freqs):
        spread(k).start()
    give(7, lines - 7)
    parts_sum = norms[...]
    for k in range(1, freqs):
        spread(k).wait_recv()
        parts_sum = parts_sum + freq_box[k]
    rcv_box[0] = parts_sum
    for k in range(1, size):
        across(k).start()
    total = parts_sum
    for k in range(1, size):
        across(k).wait_recv()
        total = total + rcv_box[k]
    step = total[0] / total[1]
    level = level_ref[0]
    for c in range(2):
        for k in range(1, freqs):
            rows_copy(c, k).wait_recv()
        rows_own(c).wait()

    def tile(i, carry):
        at = rows_at(i * 8, 8)
        for lane in range(0, picks, 128):
            c, off = lane // half, lane % half
            points = [
                (
                    pick_timed[f, at, lane : lane + 128]
                    + step * dir_timed[c, f, at, off : off + 128],
                    pick_timed[f, at, picks + lane : picks + lane + 128]
                    + step * dir_timed[c, f, at, half + off : half + off + 128],
                )
                for f in range(freqs)
            ]
            done = shrink_points(points, keep_cols[:, lane : lane + 128], level)
            for f in range(freqs):
                cols[f, at, lane : lane + 128] = done[f][0]
                cols[f, at, picks + lane : picks + lane + 128] = done[f][1]
        return carry

    lax.fori_loop(0, deep // 8, tile, 0)
    land = cols_out.at[rows_at(me * deep, deep), :]

    def cols_copy(k):
        to = (me + k) % freqs
        return pltpu.make_async_remote_copy(
            cols.at[to], land, csend.at[k], crecv.at[k],
            device_id={"freq": to}, device_id_type=MESH,
        )

    cols_own = pltpu.make_async_copy(cols.at[me], land, cown)
    for k in range(1, freqs):
        cols_copy(k).start()
    cols_own.start()
    for group in first + second + sums:
        group.drain()
    for i in range(lines):
        for k in range(1, freqs):
            forth(i, k).wait_send()
            back_copy(i, k).wait()
        back_own(i).wait()
    for k in range(1, freqs):
        spread(k).wait_send()
        for c in range(2):
            rows_copy(c, k).wait_send()
        cols_copy(k).wait()
    cols_own.wait()
    for k in range(1, size):
        across(k).wait_send()


def main_call(freqs, size, level, wave, srcs, support, green, data, shots):
    two, _, rows, width = green.shape
    picks = srcs.shape[1]
    deep = rows // freqs
    lines = deep // LINE
    f32, bf16 = jnp.float32, jnp.bfloat16
    split = jax.ShapeDtypeStruct((two, freqs, deep, width), f32)
    vmem = pltpu.VMEM
    return pl.pallas_call(
        functools.partial(main_body, freqs, size),
        out_shape=(
            split,
            split,
            jax.ShapeDtypeStruct(green.shape, f32),
            jax.ShapeDtypeStruct((rows, two * picks), f32),
            jax.ShapeDtypeStruct((two, 1, rows, picks), f32),
            jax.ShapeDtypeStruct((picks, width), bf16),
            jax.ShapeDtypeStruct((8, width), f32),
        ),
        in_specs=[SMEM, SMEM, VMEM, VMEM, ANY, ANY, ANY],
        out_specs=(ANY, ANY, ANY, ANY, VMEM, VMEM, VMEM),
        scratch_shapes=[
            vmem((two, rows, width), f32),
            vmem((two, 2, rows, width), bf16),
            vmem((2, size * rows, picks), f32),
            vmem((2, size * rows, picks), f32),
            vmem((2, size * rows, picks), f32),
            vmem((2, 2, size - 1, rows, picks), f32),
            vmem((2, rows, picks), f32),
            vmem((two, rows, picks), f32),
            vmem((rows, picks), f32),
            vmem((width, picks), bf16),
            vmem((8, width), f32),
            vmem((8, picks), f32),
            vmem((freqs, deep, two * picks), f32),
            vmem((2, freqs, deep, picks), f32),
            vmem((freqs, deep, two * picks), f32),
            vmem((2, 8, 128), f32),
            vmem((freqs, 2, 8, 128), f32),
            vmem((size, 2, 8, 128), f32),
            DMA((4,)), DMA(()), DMA(()),
            DMA((lines, freqs)), DMA((lines, freqs)), DMA(()),
            DMA((lines, freqs)), DMA((lines, freqs)), DMA((lines,)),
            DMA((6, 2, size)), DMA((6, 2, size)),
            DMA((2, freqs)), DMA((2, freqs)), DMA((2,)),
            DMA((freqs,)), DMA((freqs,)), DMA(()),
            DMA((freqs,)), DMA((freqs,)), DMA((size,)), DMA((size,)),
        ],
        compiler_params=pltpu.CompilerParams(
            collective_id=0, has_side_effects=True, vmem_limit_bytes=67043328
        ),
    )(level, wave, srcs, support, green, data, shots)


def join_body(mask_ref, hot_ref, cols_ref, back_ref, resid_ref, o_ref, r_ref):
    picks = hot_ref.shape[0]
    hot = hot_ref[...]
    mask = mask_ref[0:1, :] > 0.5
    for part in range(2):
        spread = select(cols_ref[:, part * picks : (part + 1) * picks], hot)
        o_ref[part, 0] = jnp.where(mask, spread, back_ref[part, 0])
    r_ref[...] = resid_ref[...]


def join_call(mask, hot, cols, back, resid):
    two, one, rows, width = back.shape
    picks = hot.shape[0]
    tile = rows // 8 if rows % 64 == 0 else rows
    wide = pl.BlockSpec((two, one, tile, width), lambda i: (0, 0, i, 0))
    thin = pl.BlockSpec((two, one, tile, picks), lambda i: (0, 0, i, 0))
    return pl.pallas_call(
        join_body,
        grid=(rows // tile,),
        in_specs=[
            pl.BlockSpec((8, width), lambda i: (0, 0)),
            pl.BlockSpec((picks, width), lambda i: (0, 0)),
            pl.BlockSpec((tile, two * picks), lambda i: (i, 0)),
            wide,
            thin,
        ],
        out_specs=[wide, thin],
        out_shape=[
            jax.ShapeDtypeStruct(back.shape, jnp.float32),
            jax.ShapeDtypeStruct(resid.shape, jnp.float32),
        ],
    )(mask, hot, cols, back, resid)


def pick_body(hot_ref, x_ref, o_ref):
    picks = hot_ref.shape[1]
    hot = hot_ref[...]
    for part in range(2):
        x = x_ref[part, 0]
        hi = x.astype(jnp.bfloat16)
        rest = x - hi.astype(jnp.float32)
        mid = rest.astype(jnp.bfloat16)
        low = (rest - mid.astype(jnp.float32)).astype(jnp.bfloat16)
        o_ref[:, part * picks : (part + 1) * picks] = (
            jnp.dot(hi, hot, preferred_element_type=jnp.float32)
            + jnp.dot(mid, hot, preferred_element_type=jnp.float32)
        ) + jnp.dot(low, hot, preferred_element_type=jnp.float32)


def pick_call(hot, green):
    two, one, rows, width = green.shape
    picks = hot.shape[1]
    tile = rows // 4 if rows % 32 == 0 else rows
    return pl.pallas_call(
        pick_body,
        grid=(rows // tile,),
        in_specs=[
            pl.BlockSpec((width, picks), lambda i: (0, 0)),
            pl.BlockSpec((two, one, tile, width), lambda i: (0, 0, i, 0)),
        ],
        out_specs=pl.BlockSpec((tile, 2 * picks), lambda i: (i, 0)),
        out_shape=jax.ShapeDtypeStruct((rows, 2 * picks), jnp.float32),
    )(hot, green)


def on_device(green_freq, data_matrix, shot_panels, wavelet, sources, support, threshold):
    width = green_freq.shape[3]
    rows_here = green_freq.shape[2]
    picks = sources.shape[0]
    freqs = lax.axis_size("freq")
    size = lax.axis_size("rcv")
    fast = rows_here % (LINE * freqs) == 0 and size > 2 and rows_here // freqs >= 8 * LINE
    fast = fast and rows_here % 32 == 0 and width % picks == 0 and picks % 256 == 0
    if fast:
        _, _, back, cols, resid, hot, mask = main_call(
            freqs, size, threshold, wavelet[:, 0], sources[None, :], support,
            green_freq, data_matrix, shot_panels,
        )
        green_next, residual = join_call(mask, hot, cols, back, resid)
        return (green_next, residual)
    keep_all = support.astype(jnp.float32)
    places = jnp.arange(width, dtype=jnp.int32)
    pickcat = pick_call((places[:, None] == sources[None, :]).astype(jnp.bfloat16), green_freq)
    picked = (pickcat[:, :picks], pickcat[:, picks:])
    keep_cols = jnp.take(keep_all, sources, axis=1)
    wr = wavelet[0, 0]
    wi = wavelet[1, 0]
    gathered = lax.all_to_all(green_freq, "freq", split_axis=2, concat_axis=1, tiled=True)
    both = lax.all_gather(pickcat, "rcv", axis=0, tiled=True)
    dr = data_matrix[0, 0]
    di = data_matrix[1, 0]
    flipped = jnp.concatenate([-both[:, picks:], both[:, :picks]], axis=1)
    multiple = apply_rows(dr, di, both, flipped)
    resid_real = shot_panels[0, 0] - (wr * picked[0] - wi * picked[1] - multiple[:, :picks])
    resid_imag = shot_panels[1, 0] - (wr * picked[1] + wi * picked[0] - multiple[:, picks:])
    residual = jnp.stack([resid_real, resid_imag])[:, None]
    down = ((0,), (0,))
    rboth = jnp.concatenate([resid_real, resid_imag], axis=1)
    rflip = jnp.concatenate([resid_imag, -resid_real], axis=1)
    adjoint = dots(dr, rboth, down) + dots(di, rflip, down)
    local = jnp.concatenate(
        [wr * resid_real + wi * resid_imag, wr * resid_imag - wi * resid_real], axis=1
    )
    direction = local - lax.psum_scatter(adjoint, "rcv", scatter_dimension=0, tiled=True)
    dir_all = lax.all_gather(direction, "rcv", axis=0, tiled=True)
    shrunk = shrink_call(threshold, keep_all, (gathered,))
    back = lax.all_to_all(shrunk, "freq", split_axis=1, concat_axis=2, tiled=True)
    dir_real = direction[:, :picks]
    dir_imag = direction[:, picks:]
    dir_timed = lax.all_to_all(
        jnp.stack([dir_real, dir_imag])[:, None],
        "freq", split_axis=2, concat_axis=1, tiled=True,
    )
    pushed = apply_rows(
        dr, di, dir_all, jnp.concatenate([-dir_all[:, picks:], dir_all[:, :picks]], axis=1)
    )
    image_real = wr * dir_real - wi * dir_imag - pushed[:, :picks]
    image_imag = wr * dir_imag + wi * dir_real - pushed[:, picks:]
    norm_dir = jnp.sum(direction * direction)
    norm_img = jnp.sum(image_real * image_real + image_imag * image_imag)
    totals = lax.psum(jnp.stack([norm_dir, norm_img]), ("freq", "rcv"))
    scalars = jnp.concatenate([threshold, (totals[0] / totals[1])[None]])
    pick_timed = jnp.take(gathered, sources, axis=3)
    cols = shrink_call(scalars, keep_cols, (pick_timed, dir_timed))
    cols_back = lax.all_to_all(cols, "freq", split_axis=1, concat_axis=2, tiled=True)
    cols_back = jnp.concatenate([cols_back[0, 0], cols_back[1, 0]], axis=1)
    hot = sources[:, None] == places[None, :]
    mask = jnp.any(hot, axis=0, keepdims=True).astype(jnp.float32)
    green_next = merge_call(mask, hot.astype(jnp.bfloat16), cols_back, back)
    return (green_next, residual)


def solution(mesh):
    in_specs = (
        P(None, "freq", "rcv", None),
        P(None, "freq", "rcv", None),
        P(None, "freq", "rcv", None),
        P(None, "freq"),
        P(),
        P(),
        P(),
    )
    out_specs = (P(None, "freq", "rcv", None), P(None, "freq", "rcv", None))
    return jax.shard_map(
        on_device, mesh=mesh, in_specs=in_specs, out_specs=out_specs, check_vma=False
    )
```

```python
import functools
import math

import jax
import jax.numpy as jnp
from jax import lax
from jax.experimental import pallas as pl
from jax.experimental.pallas import tpu as pltpu
from jax.sharding import PartitionSpec as P

HIGH = lax.Precision.HIGH
MESH = pl.DeviceIdType.MESH


def transform(points, sign):
    count = len(points)
    if count == 1:
        return points
    if count % 2:
        out = []
        for t in range(count):
            real, imag = points[0]
            for f in range(1, count):
                angle = sign * 2.0 * math.pi * (f * t % count) / count
                c, s = math.cos(angle), math.sin(angle)
                real = real + (c * points[f][0] - s * points[f][1])
                imag = imag + (s * points[f][0] + c * points[f][1])
            out.append((real, imag))
        return out
    even = transform(points[0::2], sign)
    odd = transform(points[1::2], sign)
    low, high = [], []
    for k in range(count // 2):
        er, ei = even[k]
        r, i = odd[k]
        angle = 8 * k / count
        if k == 0:
            tr, ti = r, i
        elif angle == 2:
            tr, ti = (-i, r) if sign > 0 else (i, -r)
        elif angle == 1:
            h = math.sqrt(0.5)
            tr, ti = (h * (r - i), h * (r + i)) if sign > 0 else (h * (r + i), h * (i - r))
        elif angle == 3:
            h = math.sqrt(0.5)
            tr, ti = (-h * (r + i), h * (r - i)) if sign > 0 else (h * (i - r), -h * (r + i))
        else:
            c = math.cos(2 * math.pi * k / count)
            s = sign * math.sin(2 * math.pi * k / count)
            tr, ti = c * r - s * i, s * r + c * i
        low.append((er + tr, ei + ti))
        high.append((er - tr, ei - ti))
    return low + high


def shrink_points(points, keep, level):
    count = len(points)
    timed = transform(points, 1)
    kept = []
    for t, (real, imag) in enumerate(timed):
        size = jnp.sqrt(real * real + imag * imag)
        factor = jnp.maximum(size - level, 0.0) / jnp.maximum(size, level) * keep[t : t + 1]
        factor = factor * (1.0 / count)
        kept.append((factor * real, factor * imag))
    return transform(kept, -1)


def shrink_body(scal_ref, keep_ref, *refs):
    *x_refs, o_ref = refs
    x_ref = x_refs[0]
    count = x_ref.shape[1]
    level = scal_ref[0]

    def lanes(j, carry):
        at = pl.ds(pl.multiple_of(j * 128, 128), 128)
        points = [(x_ref[0, f, :, at], x_ref[1, f, :, at]) for f in range(count)]
        if len(x_refs) == 2:
            d_ref = x_refs[1]
            step = scal_ref[1]
            points = [
                (r + step * d_ref[0, f, :, at], i + step * d_ref[1, f, :, at])
                for f, (r, i) in enumerate(points)
            ]
        out = shrink_points(points, keep_ref[:, at], level)
        for f in range(count):
            o_ref[0, f, :, at] = out[f][0]
            o_ref[1, f, :, at] = out[f][1]
        return carry

    lax.fori_loop(0, x_ref.shape[3] // 128, lanes, 0)


def shrink_call(scalars, keep, arrays):
    two, count, rows, width = arrays[0].shape
    tile = 8 if rows % 8 == 0 else rows
    if rows % 24 == 0 and width <= 512:
        tile = 24
    block = pl.BlockSpec((two, count, tile, width), lambda j: (0, 0, j, 0))
    size = arrays[0].size * 4
    return pl.pallas_call(
        shrink_body,
        grid=(rows // tile,),
        in_specs=[
            pl.BlockSpec(memory_space=pltpu.SMEM),
            pl.BlockSpec((count, width), lambda j: (0, 0)),
        ]
        + [block] * len(arrays),
        out_specs=block,
        out_shape=jax.ShapeDtypeStruct(arrays[0].shape, jnp.float32),
        cost_estimate=pl.CostEstimate(
            flops=40 * arrays[0].size, bytes_accessed=size * (1 + len(arrays)), transcendentals=0
        ),
    )(scalars, keep, *arrays)


def merge_body(mask_ref, hot_ref, cols_ref, back_ref, o_ref):
    hot = hot_ref[...]
    mask = mask_ref[...] > 0.5
    for part in range(2):
        x = cols_ref[:, part * hot.shape[0] : (part + 1) * hot.shape[0]]
        hi = x.astype(jnp.bfloat16)
        rest = x - hi.astype(jnp.float32)
        mid = rest.astype(jnp.bfloat16)
        low = (rest - mid.astype(jnp.float32)).astype(jnp.bfloat16)
        spread = (
            jnp.dot(hi, hot, preferred_element_type=jnp.float32)
            + jnp.dot(mid, hot, preferred_element_type=jnp.float32)
        ) + jnp.dot(low, hot, preferred_element_type=jnp.float32)
        o_ref[part, 0] = jnp.where(mask, spread, back_ref[part, 0])


def merge_call(mask, hot, cols, back):
    two, one, rows, width = back.shape
    picked = hot.shape[0]
    tile = rows // 4 if rows % 32 == 0 else rows
    return pl.pallas_call(
        merge_body,
        grid=(rows // tile,),
        in_specs=[
            pl.BlockSpec((1, width), lambda i: (0, 0)),
            pl.BlockSpec((picked, width), lambda i: (0, 0)),
            pl.BlockSpec((tile, two * picked), lambda i: (i, 0)),
            pl.BlockSpec((two, one, tile, width), lambda i: (0, 0, i, 0)),
        ],
        out_specs=pl.BlockSpec((two, one, tile, width), lambda i: (0, 0, i, 0)),
        out_shape=jax.ShapeDtypeStruct(back.shape, jnp.float32),
    )(mask, hot, cols, back)


def dots(lhs, rhs, contract):
    return lax.dot_general(lhs, rhs, (contract, ((), ())), precision=HIGH)


def apply_rows(data_real, data_imag, both, flipped):
    ahead = (((1,), (0,)))
    return dots(data_real, both, ahead) + dots(data_imag, flipped, ahead)


ANY = pl.BlockSpec(memory_space=pltpu.HBM)
VMEM = pl.BlockSpec(memory_space=pltpu.VMEM)
DMA = pltpu.SemaphoreType.DMA


SMEM = pl.BlockSpec(memory_space=pltpu.SMEM)


def halves(x):
    hi = x.astype(jnp.bfloat16)
    return hi, (x - hi.astype(jnp.float32)).astype(jnp.bfloat16)


def thirds(x):
    hi, mid = halves(x)
    rest = x - hi.astype(jnp.float32) - mid.astype(jnp.float32)
    return jnp.concatenate([hi, mid, rest.astype(jnp.bfloat16)], axis=0)


def select(x, hot):
    rows = x.shape[0]
    out = jnp.dot(thirds(x), hot, preferred_element_type=jnp.float32)
    return (out[:rows] + out[rows : 2 * rows]) + out[2 * rows :]


def spread(x, hot):
    hi, mid = halves(x)
    low = (x - hi.astype(jnp.float32) - mid.astype(jnp.float32)).astype(jnp.bfloat16)
    return (
        jnp.dot(hi, hot, preferred_element_type=jnp.float32)
        + jnp.dot(mid, hot, preferred_element_type=jnp.float32)
    ) + jnp.dot(low, hot, preferred_element_type=jnp.float32)


def six(parts, contract):
    total = None
    for (lh, ll), (rh, rl) in parts:
        for x, y in ((lh, rl), (ll, rh), (lh, rh)):
            term = lax.dot_general(
                x, y, (contract, ((), ())), preferred_element_type=jnp.float32
            )
            total = term if total is None else total + term
    return total


def piece_of(width):
    for piece in (768, 512, 256):
        if width % piece == 0:
            return piece
    return width


def apply_data(data, x_ref, acc):
    half = x_ref.shape[1] // 2
    piece = piece_of(x_ref.shape[0])
    acc[...] = jnp.zeros_like(acc)

    def chunk(i, carry):
        at = pl.ds(pl.multiple_of(i * piece, piece), piece)
        x = x_ref[at, :]
        turned = jnp.concatenate([-x[:, half:], x[:, :half]], axis=1)
        acc[...] += six(
            [
                ((data[0, 0, :, at], data[0, 1, :, at]), halves(x)),
                ((data[1, 0, :, at], data[1, 1, :, at]), halves(turned)),
            ],
            ((1,), (0,)),
        )
        return carry

    lax.fori_loop(0, x_ref.shape[0] // piece, chunk, 0)


def apply_adjoint(data, x, out):
    half = x.shape[1] // 2
    piece = piece_of(out.shape[0])
    straight = halves(x)
    turned = halves(jnp.concatenate([x[:, half:], -x[:, :half]], axis=1))

    def chunk(i, carry):
        at = pl.ds(pl.multiple_of(i * piece, piece), piece)
        out[at, :] = six(
            [
                ((data[0, 0, :, at], data[0, 1, :, at]), straight),
                ((data[1, 0, :, at], data[1, 1, :, at]), turned),
            ],
            ((0,), (0,)),
        )
        return carry

    lax.fori_loop(0, out.shape[0] // piece, chunk, 0)


class Gather:
    def __init__(self, size, buf, sends, recvs):
        self.size, self.buf, self.sends, self.recvs = size, buf, sends, recvs
        self.z = lax.axis_index("rcv")

    def ways(self, step):
        z, last = self.z, self.size - 1
        rows = self.buf.shape[0] // self.size
        for way in range(2):
            if way == 0:
                block, to = jnp.maximum(z - step, 0), jnp.minimum(z + 1, last)
                sent = (z < last) & (z >= step)
                got = z >= step + 1
            else:
                block, to = jnp.minimum(z + step, last), jnp.maximum(z - 1, 0)
                sent = (z > 0) & (z + step <= last)
                got = z + 1 + step <= last
            part = self.buf.at[pl.ds(pl.multiple_of(block * rows, 8), rows), :]
            copy = pltpu.make_async_remote_copy(
                part, part, self.sends.at[way, step], self.recvs.at[way, step],
                device_id={"rcv": to}, device_id_type=MESH,
            )
            yield copy, sent, got

    def start(self, step):
        for copy, sent, _ in self.ways(step):
            pl.when(sent)(copy.start)

    def recv(self, step):
        for copy, _, got in self.ways(step):
            pl.when(got)(copy.wait_recv)

    def drain(self):
        for step in range(self.size - 1):
            for copy, sent, _ in self.ways(step):
                pl.when(sent)(copy.wait_send)


class Scatter:
    def __init__(self, size, terms, held, sends, recvs):
        self.size, self.terms, self.held = size, terms, held
        self.sends, self.recvs = sends, recvs
        self.z = lax.axis_index("rcv")

    def ways(self, step):
        z, last = self.z, self.size - 1
        rows = self.terms.shape[0] // self.size
        for way in range(2):
            if way == 0:
                far, to = z, jnp.minimum(z + 1, last)
                block = jnp.minimum(last - step + z, last)
                more, less = z < last, z > 0
            else:
                far, to = last - z, jnp.maximum(z - 1, 0)
                block = jnp.maximum(step - last + z, 0)
                more, less = z > 0, z < last
            own = self.terms.at[pl.ds(pl.multiple_of(block * rows, 8), rows), :]
            got = less & (step >= far - 1)
            yield way, own, to, more & (far == 0), more & (far > 0) & (step >= far), got

    def copy(self, src, way, step, to):
        return pltpu.make_async_remote_copy(
            src, self.held.at[way, step], self.sends.at[way, step], self.recvs.at[way, step],
            device_id={"rcv": to}, device_id_type=MESH,
        )

    def start(self, step):
        for way, own, to, first, later, _ in self.ways(step):
            pl.when(first)(self.copy(own, way, step, to).start)
            if step:
                self.pass_on(way, own, to, step, later)

    def pass_on(self, way, own, to, step, later):
        @pl.when(later)
        def _():
            self.held[way, step - 1] = self.held[way, step - 1] + own[...]
            self.copy(self.held.at[way, step - 1], way, step, to).start()

    def recv(self, step):
        for way, own, to, _, _, got in self.ways(step):
            pl.when(got)(self.copy(own, way, step, to).wait_recv)

    def drain(self):
        for step in range(self.size - 1):
            for way, own, to, first, later, _ in self.ways(step):
                pl.when(first | later)(self.copy(own, way, step, to).wait_send)


def greet(freqs, size):
    me = lax.axis_index("freq")
    z = lax.axis_index("rcv")
    barrier = pltpu.get_barrier_semaphore()
    for k in range(1, freqs):
        pl.semaphore_signal(
            barrier, inc=1, device_id={"freq": (me + k) % freqs}, device_id_type=MESH
        )
    for k in range(1, size):
        pl.semaphore_signal(barrier, inc=1, device_id={"rcv": (z + k) % size}, device_id_type=MESH)
    pl.semaphore_wait(barrier, freqs + size - 2)


LINE = 8


def rows_at(at, count):
    return pl.ds(pl.multiple_of(at, 8), count)


def main_body(
    freqs, size, level_ref, wave, srcs, support, green, data_hbm, shots_hbm,
    gathered, shrunk, back, tails, cols_out, residual, hot_out, mask_out,
    big, data, whole, dir_all, adjoint, held, local, shots, image, hot, fill, lead,
    keep, keep_cols, timed, cols, norms, freq_box, rcv_box,
    gload, sload, load, fsend, frecv, fown, bsend, brecv, bown,
    zsend, zrecv, dsend, drecv, down, csend, crecv, cown, nfs, nfr, nzs, nzr,
):
    me = lax.axis_index("freq")
    z = lax.axis_index("rcv")
    _, _, rows, width = green.shape
    deep = rows // freqs
    lines = deep // LINE
    picks = srcs.shape[1]
    half = picks // 2
    head = width - picks
    mine = rows_at(z * rows, rows)
    parts = gload.shape[0]
    tall = rows // parts

    def loading(j):
        at = rows_at(j * tall, tall)
        return pltpu.make_async_copy(green.at[:, 0, at, :], big.at[:, at, :], gload.at[j])

    for j in range(parts):
        loading(j).start()
    fetch_shots = pltpu.make_async_copy(shots_hbm.at[:, 0], shots, sload)
    fetch_shots.start()
    slots = [box.at[c, rows_at(n * rows, rows), :]
             for box in (adjoint, dir_all) for c in range(2) for n in range(size)]
    slots += [held.at[c, way, n] for c in range(2) for way in range(2) for n in range(size - 1)]
    places = [(part, at) for part in range(2) for at in range(0, width, picks)]
    slots = slots[: len(places)]

    def fetching(n):
        part, at = places[n]
        return pltpu.make_async_copy(
            data_hbm.at[part, 0, :, pl.ds(at, picks)], slots[n], load.at[n]
        )

    for n in range(len(places)):
        fetching(n).start()

    def packed(i, to):
        if isinstance(i, int) and i == 0:
            return lead.at[:, rows_at(to * LINE, LINE), :]
        return big.at[:, rows_at(to * deep + i * LINE, LINE), pl.ds(0, head)]

    def forth(i, k):
        to = (me + k) % freqs
        return pltpu.make_async_remote_copy(
            packed(i, to), gathered.at[:, me, rows_at(i * LINE, LINE), :],
            fsend.at[i, k], frecv.at[i, k],
            device_id={"freq": to}, device_id_type=MESH,
        )

    def forth_own(i):
        return pltpu.make_async_copy(
            packed(i, me), gathered.at[:, me, rows_at(i * LINE, LINE), :], fown.at[i]
        )

    def send_forth(i):
        for k in range(1, freqs):
            forth(i, k).start()
        forth_own(i).start()

    place = lax.broadcasted_iota(jnp.int32, (width, picks), 0)
    hot[...] = jnp.where(place == srcs[...], 1.0, 0.0).astype(jnp.bfloat16)
    before = jnp.where(srcs[...] < place, 1.0, 0.0)
    ones = jnp.ones((8, picks), jnp.bfloat16)
    across_lanes = (((1,), (1,)), ((), ()))
    mask_out[...] = lax.dot_general(
        ones, hot[...], across_lanes, preferred_element_type=jnp.float32
    )
    rank = lax.dot_general(
        ones, before.astype(jnp.bfloat16), across_lanes, preferred_element_type=jnp.float32
    )
    ends = jnp.sum(before[head:, :], axis=1, keepdims=True)
    spare = 1.0 - jnp.sum(
        hot[head:, :].astype(jnp.float32), axis=1, keepdims=True
    )
    order = lax.broadcasted_iota(jnp.int32, (picks, 1), 0).astype(jnp.float32)
    order = order - (ends - ends[0:1, :])
    taken = mask_out[0:1, :head] > 0.5
    fill[...] = jnp.where(
        taken & (spare > 0.5) & (rank[0:1, :head] == order), 1.0, 0.0
    ).astype(jnp.bfloat16)

    def pack(x):
        got = spread(x[:, head:], fill[...])
        return jnp.where(mask_out[0:1, :head] > 0.5, got, x[:, :head])

    def line_of(i):
        return jnp.concatenate(
            [big[part, rows_at(o * deep + i * LINE, LINE), :] for part in range(2)
             for o in range(freqs)], axis=0,
        )

    for j in range(parts):
        loading(j).wait()
    lead_rows = pack(line_of(0))
    for part in range(2):
        lead[part] = lead_rows[part * freqs * LINE : (part + 1) * freqs * LINE]
    keep_all = support[...].astype(jnp.float32)
    keep[...] = jnp.where(
        taken,
        jnp.dot(
            keep_all[:, head:].astype(jnp.bfloat16), fill[...], preferred_element_type=jnp.float32
        ),
        keep_all[:, :head],
    )
    keep_cols[...] = jnp.dot(
        keep_all.astype(jnp.bfloat16), hot[...], preferred_element_type=jnp.float32
    )
    greet(freqs, size)
    send_forth(0)

    def pick(j, carry):
        at = rows_at(j * tall, tall)
        for part in range(2):
            out = select(big[part, at, :], hot[...])
            to = rows_at(z * rows + j * tall, tall)
            for c in range(2):
                whole[c, to, part * half : (part + 1) * half] = out[:, c * half : (c + 1) * half]
        return carry

    lax.fori_loop(0, parts, pick, 0)
    for n, (part, at) in enumerate(places):
        fetching(n).wait()
        for row in range(0, rows, rows // 2):
            there = slice(row, row + rows // 2)
            hi, lo = halves(slots[n][there, :])
            data[part, 0, there, at : at + picks] = hi
            data[part, 1, there, at : at + picks] = lo

    first = [Gather(size, whole.at[c], zsend.at[c], zrecv.at[c]) for c in range(2)]
    second = [Gather(size, dir_all.at[c], zsend.at[2 + c], zrecv.at[2 + c]) for c in range(2)]
    sums = [
        Scatter(size, adjoint.at[c], held.at[c], zsend.at[4 + c], zrecv.at[4 + c])
        for c in range(2)
    ]
    last = size - 2
    first[0].start(0)
    def pack_line(i, carry):
        done = pack(line_of(i))
        for part in range(2):
            for o in range(freqs):
                row = (part * freqs + o) * LINE
                big[part, rows_at(o * deep + i * LINE, LINE), 0:head] = done[row : row + LINE]
        return carry

    lax.fori_loop(1, lines, pack_line, 0)
    for i in range(1, lines):
        send_forth(i)
    for at in range(0, width, picks):
        hot_out[:, at : at + picks] = hot[at : at + picks, :].astype(jnp.float32).T.astype(
            jnp.bfloat16
        )

    def shrink(lo, count):
        for i in range(lo, lo + count):
            for k in range(1, freqs):
                forth(i, k).wait_recv()
            forth_own(i).wait()
        block = pl.BlockSpec((2, freqs, LINE, head), lambda j: (0, 0, lo + j, 0))
        pltpu.emit_pipeline(
            lambda x, o: shrink_body(level_ref, keep, x, o),
            grid=(count,), in_specs=[block], out_specs=[block],
        )(gathered, shrunk)

    def back_copy(i, k):
        to = (me + k) % freqs
        return pltpu.make_async_remote_copy(
            shrunk.at[:, to, pl.ds(i * LINE, LINE), :],
            back.at[:, 0, rows_at(me * deep + i * LINE, LINE), :],
            bsend.at[i, k], brecv.at[i, k],
            device_id={"freq": to}, device_id_type=MESH,
        )

    def back_own(i):
        return pltpu.make_async_copy(
            shrunk.at[:, me, pl.ds(i * LINE, LINE), :],
            back.at[:, 0, rows_at(me * deep + i * LINE, LINE), :],
            bown.at[i],
        )

    def give(lo, count):
        for i in range(lo, lo + count):
            for k in range(1, freqs):
                back_copy(i, k).start()
            back_own(i).start()

    def rows_copy(c, k):
        to = (me + k) % freqs
        return pltpu.make_async_remote_copy(
            local.at[c, rows_at(to * deep, deep), :], timed.at[c, me],
            dsend.at[c, k], drecv.at[c, k],
            device_id={"freq": to}, device_id_type=MESH,
        )

    def rows_own(c):
        return pltpu.make_async_copy(
            local.at[c, rows_at(me * deep, deep), :], timed.at[c, me], down.at[c]
        )

    wr, wi = wave[0], wave[1]
    re, im = slice(0, half), slice(half, 2 * half)

    def residual_of(c):
        apply_data(data, whole.at[c], image)
        at = slice(c * half, (c + 1) * half)
        pr, pi = whole[c, mine, re], whole[c, mine, im]
        rr = shots[0, :, at] - (wr * pr - wi * pi - image[:, re])
        ri = shots[1, :, at] - (wr * pi + wi * pr - image[:, im])
        residual[0, 0, :, at] = rr
        residual[1, 0, :, at] = ri
        local[c, :, re] = wr * rr + wi * ri
        local[c, :, im] = wr * ri - wi * rr
        apply_adjoint(data, jnp.concatenate([rr, ri], axis=1), adjoint.at[c])

    def direction_of(c):
        dir_all[c, mine, :] = local[c] - adjoint[c, mine, :]

        @pl.when(z > 0)
        def _():
            dir_all[c, mine, :] = dir_all[c, mine, :] - held[c, 0, last]

        @pl.when(z < size - 1)
        def _():
            dir_all[c, mine, :] = dir_all[c, mine, :] - held[c, 1, last]

    def send_update(c, step):
        local[c] = whole[c, mine, :] + step * dir_all[c, mine, :]
        for k in range(1, freqs):
            rows_copy(c, k).start()
        rows_own(c).start()

    def image_of(c):
        apply_data(data, dir_all.at[c], image)
        dr, di = dir_all[c, mine, re], dir_all[c, mine, im]
        gr = wr * dr - wi * di - image[:, re]
        gi = wr * di + wi * dr - image[:, im]
        return jnp.sum(dr * dr + di * di), jnp.sum(gr * gr + gi * gi)

    first[0].recv(0)
    first[0].start(1)
    fetch_shots.wait()
    first[0].recv(1)
    first[0].start(2)
    first[1].start(0)
    shrink(0, 2)
    first[0].recv(2)
    residual_of(0)
    sums[0].start(0)
    first[1].recv(0)
    first[1].start(1)
    shrink(2, 2)
    sums[0].recv(0)
    sums[0].start(1)
    first[1].recv(1)
    first[1].start(2)
    shrink(4, 1)
    sums[0].recv(1)
    sums[0].start(2)
    first[1].recv(2)
    residual_of(1)
    sums[1].start(0)
    sums[0].recv(2)
    direction_of(0)
    second[0].start(0)
    shrink(5, 2)
    give(0, 3)
    sums[1].recv(0)
    sums[1].start(1)
    second[0].recv(0)
    second[0].start(1)
    shrink(7, 1)
    give(3, 1)
    sums[1].recv(1)
    sums[1].start(2)
    second[0].recv(1)
    second[0].start(2)
    shrink(8, lines - 8)
    give(4, 1)
    sums[1].recv(2)
    direction_of(1)
    second[1].start(0)
    second[0].recv(2)
    first_norms = image_of(0)
    give(5, 1)
    second[1].recv(0)
    second[1].start(1)
    give(6, 1)
    second[1].recv(1)
    second[1].start(2)
    give(7, lines - 7)
    second[1].recv(2)
    second_norms = image_of(1)

    for n in range(2):
        norms[n] = jnp.full((8, 128), first_norms[n] + second_norms[n])

    def along(k):
        return pltpu.make_async_remote_copy(
            norms, freq_box.at[k], nfs.at[k], nfr.at[k],
            device_id={"freq": (me + k) % freqs}, device_id_type=MESH,
        )

    def across(k):
        return pltpu.make_async_remote_copy(
            rcv_box.at[0], rcv_box.at[k], nzs.at[k], nzr.at[k],
            device_id={"rcv": (z + k) % size}, device_id_type=MESH,
        )

    for k in range(1, freqs):
        along(k).start()
    parts_sum = norms[...]
    for k in range(1, freqs):
        along(k).wait_recv()
        parts_sum = parts_sum + freq_box[k]
    rcv_box[0] = parts_sum
    for k in range(1, size):
        across(k).start()
    total = parts_sum
    for k in range(1, size):
        across(k).wait_recv()
        total = total + rcv_box[k]
    step = total[0] / total[1]
    level = level_ref[0]
    for c in range(2):
        send_update(c, step[0:1, 0:1])

    def cols_copy(c, k):
        to = (me + k) % freqs
        return pltpu.make_async_remote_copy(
            cols.at[c, to], cols_out.at[rows_at(me * deep, deep), pl.ds(c * picks, picks)],
            csend.at[c, k], crecv.at[c, k],
            device_id={"freq": to}, device_id_type=MESH,
        )

    def cols_own(c):
        return pltpu.make_async_copy(
            cols.at[c, me], cols_out.at[rows_at(me * deep, deep), pl.ds(c * picks, picks)],
            cown.at[c],
        )

    for c in range(2):
        for k in range(1, freqs):
            rows_copy(c, k).wait_recv()
        rows_own(c).wait()

        def tile(i, carry):
            at = rows_at(i * 8, 8)
            for lane in range(0, half, 128):
                points = [
                    (timed[c, f, at, lane : lane + 128],
                     timed[c, f, at, half + lane : half + lane + 128])
                    for f in range(freqs)
                ]
                good = keep_cols[:, c * half + lane : c * half + lane + 128]
                done = shrink_points(points, good, level)
                for f in range(freqs):
                    cols[c, f, at, lane : lane + 128] = done[f][0]
                    cols[c, f, at, half + lane : half + lane + 128] = done[f][1]
            return carry

        lax.fori_loop(0, deep // 8, tile, 0)
        for k in range(1, freqs):
            cols_copy(c, k).start()
        cols_own(c).start()
    for i in range(lines):
        for k in range(1, freqs):
            back_copy(i, k).wait()
        back_own(i).wait()

    def tail(x_ref, o_ref):
        x = jnp.concatenate([x_ref[0, 0], x_ref[1, 0]], axis=0)
        n = x.shape[0]
        out = lax.dot_general(
            thirds(x), fill[...], across_lanes, preferred_element_type=jnp.float32
        )
        out = (out[:n] + out[n : 2 * n]) + out[2 * n :]
        o_ref[0, 0] = out[: n // 2]
        o_ref[1, 0] = out[n // 2 :]

    pltpu.emit_pipeline(
        tail, grid=(rows // deep,),
        in_specs=[pl.BlockSpec((2, 1, deep, head), lambda j: (0, 0, j, 0))],
        out_specs=[pl.BlockSpec((2, 1, deep, picks), lambda j: (0, 0, j, 0))],
    )(back, tails)
    for group in first + second + sums:
        group.drain()
    for i in range(lines):
        for k in range(1, freqs):
            forth(i, k).wait_send()
    for k in range(1, freqs):
        along(k).wait_send()
        for c in range(2):
            rows_copy(c, k).wait_send()
            cols_copy(c, k).wait()
    for c in range(2):
        cols_own(c).wait()
    for k in range(1, size):
        across(k).wait_send()


def main_call(freqs, size, level, wave, srcs, support, green, data, shots):
    two, _, rows, width = green.shape
    picks = srcs.shape[1]
    deep = rows // freqs
    lines = deep // LINE
    f32, bf16 = jnp.float32, jnp.bfloat16
    split = jax.ShapeDtypeStruct((two, freqs, deep, width - picks), f32)
    vmem = pltpu.VMEM
    return pl.pallas_call(
        functools.partial(main_body, freqs, size),
        out_shape=(
            split,
            split,
            jax.ShapeDtypeStruct((two, 1, rows, width - picks), f32),
            jax.ShapeDtypeStruct((two, 1, rows, picks), f32),
            jax.ShapeDtypeStruct((rows, two * picks), f32),
            jax.ShapeDtypeStruct((two, 1, rows, picks), f32),
            jax.ShapeDtypeStruct((picks, width), bf16),
            jax.ShapeDtypeStruct((8, width), f32),
        ),
        in_specs=[SMEM, SMEM, VMEM, VMEM, ANY, ANY, ANY],
        out_specs=(ANY, ANY, ANY, ANY, ANY, VMEM, VMEM, VMEM),
        scratch_shapes=[
            vmem((two, rows, width), f32),
            vmem((two, 2, rows, width), bf16),
            vmem((2, size * rows, picks), f32),
            vmem((2, size * rows, picks), f32),
            vmem((2, size * rows, picks), f32),
            vmem((2, 2, size - 1, rows, picks), f32),
            vmem((2, rows, picks), f32),
            vmem((two, rows, picks), f32),
            vmem((rows, picks), f32),
            vmem((width, picks), bf16),
            vmem((picks, width - picks), bf16),
            vmem((two, freqs * LINE, width - picks), f32),
            vmem((8, width - picks), f32),
            vmem((8, picks), f32),
            vmem((2, freqs, deep, picks), f32),
            vmem((2, freqs, deep, picks), f32),
            vmem((2, 8, 128), f32),
            vmem((freqs, 2, 8, 128), f32),
            vmem((size, 2, 8, 128), f32),
            DMA((4,)), DMA(()), DMA((2 * (width // picks),)),
            DMA((lines, freqs)), DMA((lines, freqs)), DMA((lines,)),
            DMA((lines, freqs)), DMA((lines, freqs)), DMA((lines,)),
            DMA((6, 2, size)), DMA((6, 2, size)),
            DMA((2, freqs)), DMA((2, freqs)), DMA((2,)),
            DMA((2, freqs)), DMA((2, freqs)), DMA((2,)),
            DMA((freqs,)), DMA((freqs,)), DMA((size,)), DMA((size,)),
        ],
        compiler_params=pltpu.CompilerParams(
            collective_id=0, has_side_effects=True, vmem_limit_bytes=67043328
        ),
    )(level, wave, srcs, support, green, data, shots)


def join_body(mask_ref, hot_ref, cols_ref, back_ref, tail_ref, resid_ref, o_ref, r_ref):
    picks = hot_ref.shape[0]
    half = picks // 2
    rows = cols_ref.shape[0]
    mask = mask_ref[0:1, :] > 0.5
    both = [
        jnp.concatenate(
            [cols_ref[:, at : at + half], cols_ref[:, picks + at : picks + at + half]], axis=1
        )
        for at in (0, half)
    ]
    wide = spread(jnp.concatenate(both, axis=0), hot_ref[...])
    for part in range(2):
        new = wide[part * rows : (part + 1) * rows]
        head = back_ref.shape[3]
        o_ref[part, 0, :, :head] = jnp.where(mask[:, :head], new[:, :head], back_ref[part, 0])
        o_ref[part, 0, :, head:] = jnp.where(mask[:, head:], new[:, head:], tail_ref[part, 0])
    r_ref[...] = resid_ref[...]


def join_call(mask, hot, cols, back, tails, resid):
    two, one, rows, head = back.shape
    picks, width = hot.shape
    tile = rows // 4 if rows % 32 == 0 else rows
    wide = pl.BlockSpec((two, one, tile, width), lambda i: (0, 0, i, 0))
    thin = pl.BlockSpec((two, one, tile, picks), lambda i: (0, 0, i, 0))
    return pl.pallas_call(
        join_body,
        grid=(rows // tile,),
        in_specs=[
            pl.BlockSpec((8, width), lambda i: (0, 0)),
            pl.BlockSpec((picks, width), lambda i: (0, 0)),
            pl.BlockSpec((tile, two * picks), lambda i: (i, 0)),
            pl.BlockSpec((two, one, tile, head), lambda i: (0, 0, i, 0)),
            thin,
            thin,
        ],
        out_specs=[wide, thin],
        out_shape=[
            jax.ShapeDtypeStruct((two, one, rows, width), jnp.float32),
            jax.ShapeDtypeStruct(resid.shape, jnp.float32),
        ],
    )(mask, hot, cols, back, tails, resid)


def pick_body(hot_ref, x_ref, o_ref):
    picks = hot_ref.shape[1]
    hot = hot_ref[...]
    for part in range(2):
        x = x_ref[part, 0]
        hi = x.astype(jnp.bfloat16)
        rest = x - hi.astype(jnp.float32)
        mid = rest.astype(jnp.bfloat16)
        low = (rest - mid.astype(jnp.float32)).astype(jnp.bfloat16)
        o_ref[:, part * picks : (part + 1) * picks] = (
            jnp.dot(hi, hot, preferred_element_type=jnp.float32)
            + jnp.dot(mid, hot, preferred_element_type=jnp.float32)
        ) + jnp.dot(low, hot, preferred_element_type=jnp.float32)


def pick_call(hot, green):
    two, one, rows, width = green.shape
    picks = hot.shape[1]
    tile = rows // 4 if rows % 32 == 0 else rows
    return pl.pallas_call(
        pick_body,
        grid=(rows // tile,),
        in_specs=[
            pl.BlockSpec((width, picks), lambda i: (0, 0)),
            pl.BlockSpec((two, one, tile, width), lambda i: (0, 0, i, 0)),
        ],
        out_specs=pl.BlockSpec((tile, 2 * picks), lambda i: (i, 0)),
        out_shape=jax.ShapeDtypeStruct((rows, 2 * picks), jnp.float32),
    )(hot, green)


def on_device(green_freq, data_matrix, shot_panels, wavelet, sources, support, threshold):
    width = green_freq.shape[3]
    rows_here = green_freq.shape[2]
    picks = sources.shape[0]
    freqs = lax.axis_size("freq")
    size = lax.axis_size("rcv")
    fast = rows_here % (LINE * freqs) == 0 and size > 2 and rows_here // freqs >= 8 * LINE
    fast = fast and rows_here % 32 == 0 and width % picks == 0 and picks % 256 == 0
    fast = fast and 2 * (width // picks) <= 8 * size - 4
    if fast:
        _, _, back, tails, cols, resid, hot, mask = main_call(
            freqs, size, threshold, wavelet[:, 0], sources[None, :], support,
            green_freq, data_matrix, shot_panels,
        )
        green_next, residual = join_call(mask, hot, cols, back, tails, resid)
        return (green_next, residual)
    keep_all = support.astype(jnp.float32)
    places = jnp.arange(width, dtype=jnp.int32)
    pickcat = pick_call((places[:, None] == sources[None, :]).astype(jnp.bfloat16), green_freq)
    picked = (pickcat[:, :picks], pickcat[:, picks:])
    keep_cols = jnp.take(keep_all, sources, axis=1)
    wr = wavelet[0, 0]
    wi = wavelet[1, 0]
    gathered = lax.all_to_all(green_freq, "freq", split_axis=2, concat_axis=1, tiled=True)
    both = lax.all_gather(pickcat, "rcv", axis=0, tiled=True)
    dr = data_matrix[0, 0]
    di = data_matrix[1, 0]
    flipped = jnp.concatenate([-both[:, picks:], both[:, :picks]], axis=1)
    multiple = apply_rows(dr, di, both, flipped)
    resid_real = shot_panels[0, 0] - (wr * picked[0] - wi * picked[1] - multiple[:, :picks])
    resid_imag = shot_panels[1, 0] - (wr * picked[1] + wi * picked[0] - multiple[:, picks:])
    residual = jnp.stack([resid_real, resid_imag])[:, None]
    down = ((0,), (0,))
    rboth = jnp.concatenate([resid_real, resid_imag], axis=1)
    rflip = jnp.concatenate([resid_imag, -resid_real], axis=1)
    adjoint = dots(dr, rboth, down) + dots(di, rflip, down)
    local = jnp.concatenate(
        [wr * resid_real + wi * resid_imag, wr * resid_imag - wi * resid_real], axis=1
    )
    direction = local - lax.psum_scatter(adjoint, "rcv", scatter_dimension=0, tiled=True)
    dir_all = lax.all_gather(direction, "rcv", axis=0, tiled=True)
    shrunk = shrink_call(threshold, keep_all, (gathered,))
    back = lax.all_to_all(shrunk, "freq", split_axis=1, concat_axis=2, tiled=True)
    dir_real = direction[:, :picks]
    dir_imag = direction[:, picks:]
    dir_timed = lax.all_to_all(
        jnp.stack([dir_real, dir_imag])[:, None],
        "freq", split_axis=2, concat_axis=1, tiled=True,
    )
    pushed = apply_rows(
        dr, di, dir_all, jnp.concatenate([-dir_all[:, picks:], dir_all[:, :picks]], axis=1)
    )
    image_real = wr * dir_real - wi * dir_imag - pushed[:, :picks]
    image_imag = wr * dir_imag + wi * dir_real - pushed[:, picks:]
    norm_dir = jnp.sum(direction * direction)
    norm_img = jnp.sum(image_real * image_real + image_imag * image_imag)
    totals = lax.psum(jnp.stack([norm_dir, norm_img]), ("freq", "rcv"))
    scalars = jnp.concatenate([threshold, (totals[0] / totals[1])[None]])
    pick_timed = jnp.take(gathered, sources, axis=3)
    cols = shrink_call(scalars, keep_cols, (pick_timed, dir_timed))
    cols_back = lax.all_to_all(cols, "freq", split_axis=1, concat_axis=2, tiled=True)
    cols_back = jnp.concatenate([cols_back[0, 0], cols_back[1, 0]], axis=1)
    hot = sources[:, None] == places[None, :]
    mask = jnp.any(hot, axis=0, keepdims=True).astype(jnp.float32)
    green_next = merge_call(mask, hot.astype(jnp.bfloat16), cols_back, back)
    return (green_next, residual)


def solution(mesh):
    in_specs = (
        P(None, "freq", "rcv", None),
        P(None, "freq", "rcv", None),
        P(None, "freq", "rcv", None),
        P(None, "freq"),
        P(),
        P(),
        P(),
    )
    out_specs = (P(None, "freq", "rcv", None), P(None, "freq", "rcv", None))
    return jax.shard_map(
        on_device, mesh=mesh, in_specs=in_specs, out_specs=out_specs, check_vma=False
    )
```

```python
import functools
import math

import jax
import jax.numpy as jnp
from jax import lax
from jax.experimental import pallas as pl
from jax.experimental.pallas import tpu as pltpu
from jax.sharding import PartitionSpec as P

HIGH = lax.Precision.HIGH
MESH = pl.DeviceIdType.MESH


def transform(points, sign):
    count = len(points)
    if count == 1:
        return points
    if count % 2:
        out = []
        for t in range(count):
            real, imag = points[0]
            for f in range(1, count):
                angle = sign * 2.0 * math.pi * (f * t % count) / count
                c, s = math.cos(angle), math.sin(angle)
                real = real + (c * points[f][0] - s * points[f][1])
                imag = imag + (s * points[f][0] + c * points[f][1])
            out.append((real, imag))
        return out
    even = transform(points[0::2], sign)
    odd = transform(points[1::2], sign)
    low, high = [], []
    for k in range(count // 2):
        er, ei = even[k]
        r, i = odd[k]
        angle = 8 * k / count
        if k == 0:
            tr, ti = r, i
        elif angle == 2:
            tr, ti = (-i, r) if sign > 0 else (i, -r)
        elif angle == 1:
            h = math.sqrt(0.5)
            tr, ti = (h * (r - i), h * (r + i)) if sign > 0 else (h * (r + i), h * (i - r))
        elif angle == 3:
            h = math.sqrt(0.5)
            tr, ti = (-h * (r + i), h * (r - i)) if sign > 0 else (h * (i - r), -h * (r + i))
        else:
            c = math.cos(2 * math.pi * k / count)
            s = sign * math.sin(2 * math.pi * k / count)
            tr, ti = c * r - s * i, s * r + c * i
        low.append((er + tr, ei + ti))
        high.append((er - tr, ei - ti))
    return low + high


def shrink_points(points, keep, level):
    count = len(points)
    timed = transform(points, 1)
    kept = []
    for t, (real, imag) in enumerate(timed):
        size = jnp.sqrt(real * real + imag * imag)
        factor = jnp.maximum(size - level, 0.0) / jnp.maximum(size, level) * keep[t : t + 1]
        factor = factor * (1.0 / count)
        kept.append((factor * real, factor * imag))
    return transform(kept, -1)


def shrink_body(scal_ref, keep_ref, *refs):
    *x_refs, o_ref = refs
    x_ref = x_refs[0]
    count = x_ref.shape[1]
    level = scal_ref[0]

    def lanes(j, carry):
        at = pl.ds(pl.multiple_of(j * 128, 128), 128)
        points = [(x_ref[0, f, :, at], x_ref[1, f, :, at]) for f in range(count)]
        if len(x_refs) == 2:
            d_ref = x_refs[1]
            step = scal_ref[1]
            points = [
                (r + step * d_ref[0, f, :, at], i + step * d_ref[1, f, :, at])
                for f, (r, i) in enumerate(points)
            ]
        out = shrink_points(points, keep_ref[:, at], level)
        for f in range(count):
            o_ref[0, f, :, at] = out[f][0]
            o_ref[1, f, :, at] = out[f][1]
        return carry

    lax.fori_loop(0, x_ref.shape[3] // 128, lanes, 0)


def shrink_call(scalars, keep, arrays):
    two, count, rows, width = arrays[0].shape
    tile = 8 if rows % 8 == 0 else rows
    if rows % 24 == 0 and width <= 512:
        tile = 24
    block = pl.BlockSpec((two, count, tile, width), lambda j: (0, 0, j, 0))
    size = arrays[0].size * 4
    return pl.pallas_call(
        shrink_body,
        grid=(rows // tile,),
        in_specs=[
            pl.BlockSpec(memory_space=pltpu.SMEM),
            pl.BlockSpec((count, width), lambda j: (0, 0)),
        ]
        + [block] * len(arrays),
        out_specs=block,
        out_shape=jax.ShapeDtypeStruct(arrays[0].shape, jnp.float32),
        cost_estimate=pl.CostEstimate(
            flops=40 * arrays[0].size, bytes_accessed=size * (1 + len(arrays)), transcendentals=0
        ),
    )(scalars, keep, *arrays)


def merge_body(mask_ref, hot_ref, cols_ref, back_ref, o_ref):
    hot = hot_ref[...]
    mask = mask_ref[...] > 0.5
    for part in range(2):
        x = cols_ref[:, part * hot.shape[0] : (part + 1) * hot.shape[0]]
        hi = x.astype(jnp.bfloat16)
        rest = x - hi.astype(jnp.float32)
        mid = rest.astype(jnp.bfloat16)
        low = (rest - mid.astype(jnp.float32)).astype(jnp.bfloat16)
        spread = (
            jnp.dot(hi, hot, preferred_element_type=jnp.float32)
            + jnp.dot(mid, hot, preferred_element_type=jnp.float32)
        ) + jnp.dot(low, hot, preferred_element_type=jnp.float32)
        o_ref[part, 0] = jnp.where(mask, spread, back_ref[part, 0])


def merge_call(mask, hot, cols, back):
    two, one, rows, width = back.shape
    picked = hot.shape[0]
    tile = rows // 4 if rows % 32 == 0 else rows
    return pl.pallas_call(
        merge_body,
        grid=(rows // tile,),
        in_specs=[
            pl.BlockSpec((1, width), lambda i: (0, 0)),
            pl.BlockSpec((picked, width), lambda i: (0, 0)),
            pl.BlockSpec((tile, two * picked), lambda i: (i, 0)),
            pl.BlockSpec((two, one, tile, width), lambda i: (0, 0, i, 0)),
        ],
        out_specs=pl.BlockSpec((two, one, tile, width), lambda i: (0, 0, i, 0)),
        out_shape=jax.ShapeDtypeStruct(back.shape, jnp.float32),
    )(mask, hot, cols, back)


def dots(lhs, rhs, contract):
    return lax.dot_general(lhs, rhs, (contract, ((), ())), precision=HIGH)


def apply_rows(data_real, data_imag, both, flipped):
    ahead = (((1,), (0,)))
    return dots(data_real, both, ahead) + dots(data_imag, flipped, ahead)


ANY = pl.BlockSpec(memory_space=pltpu.HBM)
VMEM = pl.BlockSpec(memory_space=pltpu.VMEM)
DMA = pltpu.SemaphoreType.DMA


SMEM = pl.BlockSpec(memory_space=pltpu.SMEM)


def halves(x):
    hi = x.astype(jnp.bfloat16)
    return hi, (x - hi.astype(jnp.float32)).astype(jnp.bfloat16)


def thirds(x):
    hi, mid = halves(x)
    rest = x - hi.astype(jnp.float32) - mid.astype(jnp.float32)
    return jnp.concatenate([hi, mid, rest.astype(jnp.bfloat16)], axis=0)


def select(x, hot):
    rows = x.shape[0]
    out = jnp.dot(thirds(x), hot, preferred_element_type=jnp.float32)
    return (out[:rows] + out[rows : 2 * rows]) + out[2 * rows :]


def spread(x, hot):
    hi, mid = halves(x)
    low = (x - hi.astype(jnp.float32) - mid.astype(jnp.float32)).astype(jnp.bfloat16)
    return (
        jnp.dot(hi, hot, preferred_element_type=jnp.float32)
        + jnp.dot(mid, hot, preferred_element_type=jnp.float32)
    ) + jnp.dot(low, hot, preferred_element_type=jnp.float32)


def six(parts, contract):
    total = None
    for (lh, ll), (rh, rl) in parts:
        for x, y in ((lh, rl), (ll, rh), (lh, rh)):
            term = lax.dot_general(
                x, y, (contract, ((), ())), preferred_element_type=jnp.float32
            )
            total = term if total is None else total + term
    return total


def piece_of(width):
    for piece in (768, 512, 256):
        if width % piece == 0:
            return piece
    return width


def apply_data(data, x_ref, acc):
    half = x_ref.shape[1] // 2
    piece = piece_of(x_ref.shape[0])
    acc[...] = jnp.zeros_like(acc)

    def chunk(i, carry):
        at = pl.ds(pl.multiple_of(i * piece, piece), piece)
        x = x_ref[at, :]
        turned = jnp.concatenate([-x[:, half:], x[:, :half]], axis=1)
        acc[...] += six(
            [
                ((data[0, 0, :, at], data[0, 1, :, at]), halves(x)),
                ((data[1, 0, :, at], data[1, 1, :, at]), halves(turned)),
            ],
            ((1,), (0,)),
        )
        return carry

    lax.fori_loop(0, x_ref.shape[0] // piece, chunk, 0)


def apply_adjoint(data, x, out):
    half = x.shape[1] // 2
    piece = piece_of(out.shape[0])
    straight = halves(x)
    turned = halves(jnp.concatenate([x[:, half:], -x[:, :half]], axis=1))

    def chunk(i, carry):
        at = pl.ds(pl.multiple_of(i * piece, piece), piece)
        out[at, :] = six(
            [
                ((data[0, 0, :, at], data[0, 1, :, at]), straight),
                ((data[1, 0, :, at], data[1, 1, :, at]), turned),
            ],
            ((0,), (0,)),
        )
        return carry

    lax.fori_loop(0, out.shape[0] // piece, chunk, 0)


class Gather:
    def __init__(self, size, buf, sends, recvs):
        self.size, self.buf, self.sends, self.recvs = size, buf, sends, recvs
        self.z = lax.axis_index("rcv")

    def ways(self, step):
        z, last = self.z, self.size - 1
        rows = self.buf.shape[0] // self.size
        for way in range(2):
            if way == 0:
                block, to = jnp.maximum(z - step, 0), jnp.minimum(z + 1, last)
                sent = (z < last) & (z >= step)
                got = z >= step + 1
            else:
                block, to = jnp.minimum(z + step, last), jnp.maximum(z - 1, 0)
                sent = (z > 0) & (z + step <= last)
                got = z + 1 + step <= last
            part = self.buf.at[pl.ds(pl.multiple_of(block * rows, 8), rows), :]
            copy = pltpu.make_async_remote_copy(
                part, part, self.sends.at[way, step], self.recvs.at[way, step],
                device_id={"rcv": to}, device_id_type=MESH,
            )
            yield copy, sent, got

    def start(self, step):
        for copy, sent, _ in self.ways(step):
            pl.when(sent)(copy.start)

    def recv(self, step):
        for copy, _, got in self.ways(step):
            pl.when(got)(copy.wait_recv)

    def drain(self):
        for step in range(self.size - 1):
            for copy, sent, _ in self.ways(step):
                pl.when(sent)(copy.wait_send)


class Scatter:
    def __init__(self, size, terms, held, sends, recvs):
        self.size, self.terms, self.held = size, terms, held
        self.sends, self.recvs = sends, recvs
        self.z = lax.axis_index("rcv")

    def ways(self, step):
        z, last = self.z, self.size - 1
        rows = self.terms.shape[0] // self.size
        for way in range(2):
            if way == 0:
                far, to = z, jnp.minimum(z + 1, last)
                block = jnp.minimum(last - step + z, last)
                more, less = z < last, z > 0
            else:
                far, to = last - z, jnp.maximum(z - 1, 0)
                block = jnp.maximum(step - last + z, 0)
                more, less = z > 0, z < last
            own = self.terms.at[pl.ds(pl.multiple_of(block * rows, 8), rows), :]
            got = less & (step >= far - 1)
            yield way, own, to, more & (far == 0), more & (far > 0) & (step >= far), got

    def copy(self, src, way, step, to):
        return pltpu.make_async_remote_copy(
            src, self.held.at[way, step], self.sends.at[way, step], self.recvs.at[way, step],
            device_id={"rcv": to}, device_id_type=MESH,
        )

    def start(self, step):
        for way, own, to, first, later, _ in self.ways(step):
            pl.when(first)(self.copy(own, way, step, to).start)
            if step:
                self.pass_on(way, own, to, step, later)

    def pass_on(self, way, own, to, step, later):
        @pl.when(later)
        def _():
            self.held[way, step - 1] = self.held[way, step - 1] + own[...]
            self.copy(self.held.at[way, step - 1], way, step, to).start()

    def recv(self, step):
        for way, own, to, _, _, got in self.ways(step):
            pl.when(got)(self.copy(own, way, step, to).wait_recv)

    def drain(self):
        for step in range(self.size - 1):
            for way, own, to, first, later, _ in self.ways(step):
                pl.when(first | later)(self.copy(own, way, step, to).wait_send)


def greet(freqs, size):
    me = lax.axis_index("freq")
    z = lax.axis_index("rcv")
    barrier = pltpu.get_barrier_semaphore()
    for k in range(1, freqs):
        pl.semaphore_signal(
            barrier, inc=1, device_id={"freq": (me + k) % freqs}, device_id_type=MESH
        )
    for k in range(1, size):
        pl.semaphore_signal(barrier, inc=1, device_id={"rcv": (z + k) % size}, device_id_type=MESH)
    pl.semaphore_wait(barrier, freqs + size - 2)


LINE = 8


def rows_at(at, count):
    return pl.ds(pl.multiple_of(at, 8), count)


def main_body(
    freqs, size, level_ref, wave, srcs, support, green, data_hbm, shots_hbm,
    gathered, shrunk, back, tails, cols_out, residual, hot_out, mask_out,
    big, data, whole, dir_all, adjoint, held, local, shots, image, hot, fill, lead,
    keep, keep_cols, timed, cols, norms, freq_box, rcv_box,
    gload, sload, load, fsend, frecv, fown, bsend, brecv, bown,
    zsend, zrecv, dsend, drecv, down, csend, crecv, cown, nfs, nfr, nzs, nzr,
):
    me = lax.axis_index("freq")
    z = lax.axis_index("rcv")
    _, _, rows, width = green.shape
    deep = rows // freqs
    lines = deep // LINE
    picks = srcs.shape[1]
    half = picks // 2
    head = width - picks
    mine = rows_at(z * rows, rows)
    parts = gload.shape[0]
    tall = rows // parts

    def loading(j):
        at = rows_at(j * tall, tall)
        return pltpu.make_async_copy(green.at[:, 0, at, :], big.at[:, at, :], gload.at[j])

    for j in range(parts):
        loading(j).start()
    fetch_shots = pltpu.make_async_copy(shots_hbm.at[:, 0], shots, sload)
    fetch_shots.start()
    slots = [box.at[c, rows_at(n * rows, rows), :]
             for box in (adjoint, dir_all) for c in range(2) for n in range(size)]
    slots += [held.at[c, way, n] for c in range(2) for way in range(2) for n in range(size - 1)]
    places = [(part, at) for part in range(2) for at in range(0, width, picks)]
    slots = slots[: len(places)]

    def fetching(n):
        part, at = places[n]
        return pltpu.make_async_copy(
            data_hbm.at[part, 0, :, pl.ds(at, picks)], slots[n], load.at[n]
        )

    for n in range(len(places)):
        fetching(n).start()

    def packed(i, to):
        if isinstance(i, int) and i == 0:
            return lead.at[:, rows_at(to * LINE, LINE), :]
        return big.at[:, rows_at(to * deep + i * LINE, LINE), pl.ds(0, head)]

    def forth(i, k):
        to = (me + k) % freqs
        return pltpu.make_async_remote_copy(
            packed(i, to), gathered.at[:, me, rows_at(i * LINE, LINE), :],
            fsend.at[i, k], frecv.at[i, k],
            device_id={"freq": to}, device_id_type=MESH,
        )

    def forth_own(i):
        return pltpu.make_async_copy(
            packed(i, me), gathered.at[:, me, rows_at(i * LINE, LINE), :], fown.at[i]
        )

    def send_forth(i):
        for k in range(1, freqs):
            forth(i, k).start()
        forth_own(i).start()

    place = lax.broadcasted_iota(jnp.int32, (width, picks), 0)
    hot[...] = jnp.where(place == srcs[...], 1.0, 0.0).astype(jnp.bfloat16)
    before = jnp.where(srcs[...] < place, 1.0, 0.0)
    ones = jnp.ones((8, picks), jnp.bfloat16)
    across_lanes = (((1,), (1,)), ((), ()))
    mask_out[...] = lax.dot_general(
        ones, hot[...], across_lanes, preferred_element_type=jnp.float32
    )
    rank = lax.dot_general(
        ones, before.astype(jnp.bfloat16), across_lanes, preferred_element_type=jnp.float32
    )
    ends = jnp.sum(before[head:, :], axis=1, keepdims=True)
    spare = 1.0 - jnp.sum(
        hot[head:, :].astype(jnp.float32), axis=1, keepdims=True
    )
    order = lax.broadcasted_iota(jnp.int32, (picks, 1), 0).astype(jnp.float32)
    order = order - (ends - ends[0:1, :])
    taken = mask_out[0:1, :head] > 0.5
    fill[...] = jnp.where(
        taken & (spare > 0.5) & (rank[0:1, :head] == order), 1.0, 0.0
    ).astype(jnp.bfloat16)

    def pack(x):
        got = spread(x[:, head:], fill[...])
        return jnp.where(mask_out[0:1, :head] > 0.5, got, x[:, :head])

    def line_of(i):
        return jnp.concatenate(
            [big[part, rows_at(o * deep + i * LINE, LINE), :] for part in range(2)
             for o in range(freqs)], axis=0,
        )

    for j in range(parts):
        loading(j).wait()
    lead_rows = pack(line_of(0))
    for part in range(2):
        lead[part] = lead_rows[part * freqs * LINE : (part + 1) * freqs * LINE]
    keep_all = support[...].astype(jnp.float32)
    keep[...] = jnp.where(
        taken,
        jnp.dot(
            keep_all[:, head:].astype(jnp.bfloat16), fill[...], preferred_element_type=jnp.float32
        ),
        keep_all[:, :head],
    )
    keep_cols[...] = jnp.dot(
        keep_all.astype(jnp.bfloat16), hot[...], preferred_element_type=jnp.float32
    )
    greet(freqs, size)
    send_forth(0)

    def pick(j, carry):
        at = rows_at(j * tall, tall)
        for part in range(2):
            out = select(big[part, at, :], hot[...])
            to = rows_at(z * rows + j * tall, tall)
            for c in range(2):
                whole[c, to, part * half : (part + 1) * half] = out[:, c * half : (c + 1) * half]
        return carry

    lax.fori_loop(0, parts, pick, 0)
    for n, (part, at) in enumerate(places):
        fetching(n).wait()
        for row in range(0, rows, rows // 2):
            there = slice(row, row + rows // 2)
            hi, lo = halves(slots[n][there, :])
            data[part, 0, there, at : at + picks] = hi
            data[part, 1, there, at : at + picks] = lo

    first = [Gather(size, whole.at[c], zsend.at[c], zrecv.at[c]) for c in range(2)]
    second = [Gather(size, dir_all.at[c], zsend.at[2 + c], zrecv.at[2 + c]) for c in range(2)]
    sums = [
        Scatter(size, adjoint.at[c], held.at[c], zsend.at[4 + c], zrecv.at[4 + c])
        for c in range(2)
    ]
    last = size - 2
    first[0].start(0)
    def pack_line(i, carry):
        done = pack(line_of(i))
        for part in range(2):
            for o in range(freqs):
                row = (part * freqs + o) * LINE
                big[part, rows_at(o * deep + i * LINE, LINE), 0:head] = done[row : row + LINE]
        return carry

    lax.fori_loop(1, lines, pack_line, 0)
    for i in range(1, lines):
        send_forth(i)
    for at in range(0, width, picks):
        hot_out[:, at : at + picks] = hot[at : at + picks, :].astype(jnp.float32).T.astype(
            jnp.bfloat16
        )

    def shrink(lo, count):
        for i in range(lo, lo + count):
            for k in range(1, freqs):
                forth(i, k).wait_recv()
            forth_own(i).wait()
        block = pl.BlockSpec((2, freqs, LINE, head), lambda j: (0, 0, lo + j, 0))
        pltpu.emit_pipeline(
            lambda x, o: shrink_body(level_ref, keep, x, o),
            grid=(count,), in_specs=[block], out_specs=[block],
        )(gathered, shrunk)

    def back_ends(i, to):
        line = min(i, lines - 1)
        part = slice(0, 2) if i < lines - 1 else slice(i - line, i - line + 1)
        return (
            shrunk.at[part, to, pl.ds(line * LINE, LINE), :],
            back.at[part, 0, rows_at(me * deep + line * LINE, LINE), :],
        )

    def back_copy(i, k):
        to = (me + k) % freqs
        return pltpu.make_async_remote_copy(
            *back_ends(i, to), bsend.at[i, k], brecv.at[i, k],
            device_id={"freq": to}, device_id_type=MESH,
        )

    def back_own(i):
        return pltpu.make_async_copy(*back_ends(i, me), bown.at[i])

    def give(lo, count):
        for i in range(lo, lo + count):
            for k in range(1, freqs):
                back_copy(i, k).start()
            back_own(i).start()

    def rows_copy(c, k):
        to = (me + k) % freqs
        return pltpu.make_async_remote_copy(
            local.at[c, rows_at(to * deep, deep), :], timed.at[c, me],
            dsend.at[c, k], drecv.at[c, k],
            device_id={"freq": to}, device_id_type=MESH,
        )

    def rows_own(c):
        return pltpu.make_async_copy(
            local.at[c, rows_at(me * deep, deep), :], timed.at[c, me], down.at[c]
        )

    wr, wi = wave[0], wave[1]
    re, im = slice(0, half), slice(half, 2 * half)

    def residual_of(c):
        apply_data(data, whole.at[c], image)
        at = slice(c * half, (c + 1) * half)
        pr, pi = whole[c, mine, re], whole[c, mine, im]
        rr = shots[0, :, at] - (wr * pr - wi * pi - image[:, re])
        ri = shots[1, :, at] - (wr * pi + wi * pr - image[:, im])
        residual[0, 0, :, at] = rr
        residual[1, 0, :, at] = ri
        local[c, :, re] = wr * rr + wi * ri
        local[c, :, im] = wr * ri - wi * rr
        apply_adjoint(data, jnp.concatenate([rr, ri], axis=1), adjoint.at[c])

    def direction_of(c):
        dir_all[c, mine, :] = local[c] - adjoint[c, mine, :]

        @pl.when(z > 0)
        def _():
            dir_all[c, mine, :] = dir_all[c, mine, :] - held[c, 0, last]

        @pl.when(z < size - 1)
        def _():
            dir_all[c, mine, :] = dir_all[c, mine, :] - held[c, 1, last]

    def send_update(c, step):
        local[c] = whole[c, mine, :] + step * dir_all[c, mine, :]
        for k in range(1, freqs):
            rows_copy(c, k).start()
        rows_own(c).start()

    def image_of(c):
        apply_data(data, dir_all.at[c], image)
        dr, di = dir_all[c, mine, re], dir_all[c, mine, im]
        gr = wr * dr - wi * di - image[:, re]
        gi = wr * di + wi * dr - image[:, im]
        return jnp.sum(dr * dr + di * di), jnp.sum(gr * gr + gi * gi)

    first[0].recv(0)
    first[0].start(1)
    fetch_shots.wait()
    first[0].recv(1)
    first[0].start(2)
    first[1].start(0)
    shrink(0, 2)
    first[0].recv(2)
    residual_of(0)
    sums[0].start(0)
    first[1].recv(0)
    first[1].start(1)
    shrink(2, 2)
    give(0, 4)
    sums[0].recv(0)
    sums[0].start(1)
    first[1].recv(1)
    first[1].start(2)
    shrink(4, 1)
    give(4, 1)
    sums[0].recv(1)
    sums[0].start(2)
    first[1].recv(2)
    residual_of(1)
    sums[1].start(0)
    sums[0].recv(2)
    direction_of(0)
    second[0].start(0)
    shrink(5, 2)
    give(5, 2)
    sums[1].recv(0)
    sums[1].start(1)
    second[0].recv(0)
    second[0].start(1)
    shrink(7, 1)
    give(7, 1)
    sums[1].recv(1)
    sums[1].start(2)
    second[0].recv(1)
    second[0].start(2)
    shrink(8, lines - 8)
    give(8, lines - 8)
    sums[1].recv(2)
    direction_of(1)
    second[1].start(0)
    second[0].recv(2)
    first_norms = image_of(0)
    second[1].recv(0)
    second[1].start(1)
    second[1].recv(1)
    second[1].start(2)
    second[1].recv(2)
    second_norms = image_of(1)

    for n in range(2):
        norms[n] = jnp.full((8, 128), first_norms[n] + second_norms[n])

    def along(k):
        return pltpu.make_async_remote_copy(
            norms, freq_box.at[k], nfs.at[k], nfr.at[k],
            device_id={"freq": (me + k) % freqs}, device_id_type=MESH,
        )

    def across(k):
        return pltpu.make_async_remote_copy(
            rcv_box.at[0], rcv_box.at[k], nzs.at[k], nzr.at[k],
            device_id={"rcv": (z + k) % size}, device_id_type=MESH,
        )

    for k in range(1, freqs):
        along(k).start()
    give(lines, 1)
    parts_sum = norms[...]
    for k in range(1, freqs):
        along(k).wait_recv()
        parts_sum = parts_sum + freq_box[k]
    rcv_box[0] = parts_sum
    for k in range(1, size):
        across(k).start()
    total = parts_sum
    for k in range(1, size):
        across(k).wait_recv()
        total = total + rcv_box[k]
    step = total[0] / total[1]
    level = level_ref[0]
    for c in range(2):
        send_update(c, step[0:1, 0:1])

    def cols_copy(c, k):
        to = (me + k) % freqs
        return pltpu.make_async_remote_copy(
            cols.at[c, to], cols_out.at[rows_at(me * deep, deep), pl.ds(c * picks, picks)],
            csend.at[c, k], crecv.at[c, k],
            device_id={"freq": to}, device_id_type=MESH,
        )

    def cols_own(c):
        return pltpu.make_async_copy(
            cols.at[c, me], cols_out.at[rows_at(me * deep, deep), pl.ds(c * picks, picks)],
            cown.at[c],
        )

    for c in range(2):
        for k in range(1, freqs):
            rows_copy(c, k).wait_recv()
        rows_own(c).wait()

        def tile(i, carry):
            at = rows_at(i * 8, 8)
            for lane in range(0, half, 128):
                points = [
                    (timed[c, f, at, lane : lane + 128],
                     timed[c, f, at, half + lane : half + lane + 128])
                    for f in range(freqs)
                ]
                good = keep_cols[:, c * half + lane : c * half + lane + 128]
                done = shrink_points(points, good, level)
                for f in range(freqs):
                    cols[c, f, at, lane : lane + 128] = done[f][0]
                    cols[c, f, at, half + lane : half + lane + 128] = done[f][1]
            return carry

        lax.fori_loop(0, deep // 8, tile, 0)
        for k in range(1, freqs):
            cols_copy(c, k).start()
        cols_own(c).start()
    for i in range(lines + 1):
        for k in range(1, freqs):
            back_copy(i, k).wait()
        back_own(i).wait()

    def tail(x_ref, o_ref):
        x = jnp.concatenate([x_ref[0, 0], x_ref[1, 0]], axis=0)
        n = x.shape[0]
        out = lax.dot_general(
            thirds(x), fill[...], across_lanes, preferred_element_type=jnp.float32
        )
        out = (out[:n] + out[n : 2 * n]) + out[2 * n :]
        o_ref[0, 0] = out[: n // 2]
        o_ref[1, 0] = out[n // 2 :]

    pltpu.emit_pipeline(
        tail, grid=(rows // deep,),
        in_specs=[pl.BlockSpec((2, 1, deep, head), lambda j: (0, 0, j, 0))],
        out_specs=[pl.BlockSpec((2, 1, deep, picks), lambda j: (0, 0, j, 0))],
    )(back, tails)
    for group in first + second + sums:
        group.drain()
    for i in range(lines):
        for k in range(1, freqs):
            forth(i, k).wait_send()
    for k in range(1, freqs):
        along(k).wait_send()
        for c in range(2):
            rows_copy(c, k).wait_send()
            cols_copy(c, k).wait()
    for c in range(2):
        cols_own(c).wait()
    for k in range(1, size):
        across(k).wait_send()


def main_call(freqs, size, level, wave, srcs, support, green, data, shots):
    two, _, rows, width = green.shape
    picks = srcs.shape[1]
    deep = rows // freqs
    lines = deep // LINE
    f32, bf16 = jnp.float32, jnp.bfloat16
    split = jax.ShapeDtypeStruct((two, freqs, deep, width - picks), f32)
    vmem = pltpu.VMEM
    return pl.pallas_call(
        functools.partial(main_body, freqs, size),
        out_shape=(
            split,
            split,
            jax.ShapeDtypeStruct((two, 1, rows, width - picks), f32),
            jax.ShapeDtypeStruct((two, 1, rows, picks), f32),
            jax.ShapeDtypeStruct((rows, two * picks), f32),
            jax.ShapeDtypeStruct((two, 1, rows, picks), f32),
            jax.ShapeDtypeStruct((picks, width), bf16),
            jax.ShapeDtypeStruct((8, width), f32),
        ),
        in_specs=[SMEM, SMEM, VMEM, VMEM, ANY, ANY, ANY],
        out_specs=(ANY, ANY, ANY, ANY, ANY, VMEM, VMEM, VMEM),
        scratch_shapes=[
            vmem((two, rows, width), f32),
            vmem((two, 2, rows, width), bf16),
            vmem((2, size * rows, picks), f32),
            vmem((2, size * rows, picks), f32),
            vmem((2, size * rows, picks), f32),
            vmem((2, 2, size - 1, rows, picks), f32),
            vmem((2, rows, picks), f32),
            vmem((two, rows, picks), f32),
            vmem((rows, picks), f32),
            vmem((width, picks), bf16),
            vmem((picks, width - picks), bf16),
            vmem((two, freqs * LINE, width - picks), f32),
            vmem((8, width - picks), f32),
            vmem((8, picks), f32),
            vmem((2, freqs, deep, picks), f32),
            vmem((2, freqs, deep, picks), f32),
            vmem((2, 8, 128), f32),
            vmem((freqs, 2, 8, 128), f32),
            vmem((size, 2, 8, 128), f32),
            DMA((4,)), DMA(()), DMA((2 * (width // picks),)),
            DMA((lines, freqs)), DMA((lines, freqs)), DMA((lines,)),
            DMA((lines + 1, freqs)), DMA((lines + 1, freqs)), DMA((lines + 1,)),
            DMA((6, 2, size)), DMA((6, 2, size)),
            DMA((2, freqs)), DMA((2, freqs)), DMA((2,)),
            DMA((2, freqs)), DMA((2, freqs)), DMA((2,)),
            DMA((freqs,)), DMA((freqs,)), DMA((size,)), DMA((size,)),
        ],
        compiler_params=pltpu.CompilerParams(
            collective_id=0, has_side_effects=True, vmem_limit_bytes=67043328
        ),
    )(level, wave, srcs, support, green, data, shots)


def join_body(mask_ref, hot_ref, cols_ref, back_ref, tail_ref, resid_ref, o_ref, r_ref, stacked):
    picks = hot_ref.shape[0]
    half = picks // 2
    rows = cols_ref.shape[0]
    mask = mask_ref[0:1, :] > 0.5

    @pl.when(pl.program_id(0) == 0)
    def _():
        for n in range(3):
            stacked[n * picks : (n + 1) * picks, :] = hot_ref[...]

    both = [
        jnp.concatenate(
            [cols_ref[:, at : at + half], cols_ref[:, picks + at : picks + at + half]], axis=1
        )
        for at in (0, half)
    ]
    x = jnp.concatenate(both, axis=0)
    hi, mid = halves(x)
    low = (x - hi.astype(jnp.float32) - mid.astype(jnp.float32)).astype(jnp.bfloat16)
    wide = jnp.dot(
        jnp.concatenate([hi, mid, low], axis=1), stacked[...], preferred_element_type=jnp.float32
    )
    for part in range(2):
        new = wide[part * rows : (part + 1) * rows]
        head = back_ref.shape[3]
        o_ref[part, 0, :, :head] = jnp.where(mask[:, :head], new[:, :head], back_ref[part, 0])
        o_ref[part, 0, :, head:] = jnp.where(mask[:, head:], new[:, head:], tail_ref[part, 0])
    r_ref[...] = resid_ref[...]


def join_call(mask, hot, cols, back, tails, resid):
    two, one, rows, head = back.shape
    picks, width = hot.shape
    tile = rows // 4 if rows % 32 == 0 else rows
    wide = pl.BlockSpec((two, one, tile, width), lambda i: (0, 0, i, 0))
    thin = pl.BlockSpec((two, one, tile, picks), lambda i: (0, 0, i, 0))
    return pl.pallas_call(
        join_body,
        grid=(rows // tile,),
        in_specs=[
            pl.BlockSpec((8, width), lambda i: (0, 0)),
            pl.BlockSpec((picks, width), lambda i: (0, 0)),
            pl.BlockSpec((tile, two * picks), lambda i: (i, 0)),
            pl.BlockSpec((two, one, tile, head), lambda i: (0, 0, i, 0)),
            thin,
            thin,
        ],
        out_specs=[wide, thin],
        out_shape=[
            jax.ShapeDtypeStruct((two, one, rows, width), jnp.float32),
            jax.ShapeDtypeStruct(resid.shape, jnp.float32),
        ],
        scratch_shapes=[pltpu.VMEM((3 * picks, width), jnp.bfloat16)],
    )(mask, hot, cols, back, tails, resid)


def pick_body(hot_ref, x_ref, o_ref):
    picks = hot_ref.shape[1]
    hot = hot_ref[...]
    for part in range(2):
        x = x_ref[part, 0]
        hi = x.astype(jnp.bfloat16)
        rest = x - hi.astype(jnp.float32)
        mid = rest.astype(jnp.bfloat16)
        low = (rest - mid.astype(jnp.float32)).astype(jnp.bfloat16)
        o_ref[:, part * picks : (part + 1) * picks] = (
            jnp.dot(hi, hot, preferred_element_type=jnp.float32)
            + jnp.dot(mid, hot, preferred_element_type=jnp.float32)
        ) + jnp.dot(low, hot, preferred_element_type=jnp.float32)


def pick_call(hot, green):
    two, one, rows, width = green.shape
    picks = hot.shape[1]
    tile = rows // 4 if rows % 32 == 0 else rows
    return pl.pallas_call(
        pick_body,
        grid=(rows // tile,),
        in_specs=[
            pl.BlockSpec((width, picks), lambda i: (0, 0)),
            pl.BlockSpec((two, one, tile, width), lambda i: (0, 0, i, 0)),
        ],
        out_specs=pl.BlockSpec((tile, 2 * picks), lambda i: (i, 0)),
        out_shape=jax.ShapeDtypeStruct((rows, 2 * picks), jnp.float32),
    )(hot, green)


def on_device(green_freq, data_matrix, shot_panels, wavelet, sources, support, threshold):
    width = green_freq.shape[3]
    rows_here = green_freq.shape[2]
    picks = sources.shape[0]
    freqs = lax.axis_size("freq")
    size = lax.axis_size("rcv")
    fast = rows_here % (LINE * freqs) == 0 and size > 2 and rows_here // freqs >= 9 * LINE
    fast = fast and rows_here % 32 == 0 and width % picks == 0 and picks % 256 == 0
    fast = fast and 2 * (width // picks) <= 8 * size - 4
    if fast:
        _, _, back, tails, cols, resid, hot, mask = main_call(
            freqs, size, threshold, wavelet[:, 0], sources[None, :], support,
            green_freq, data_matrix, shot_panels,
        )
        green_next, residual = join_call(mask, hot, cols, back, tails, resid)
        return (green_next, residual)
    keep_all = support.astype(jnp.float32)
    places = jnp.arange(width, dtype=jnp.int32)
    pickcat = pick_call((places[:, None] == sources[None, :]).astype(jnp.bfloat16), green_freq)
    picked = (pickcat[:, :picks], pickcat[:, picks:])
    keep_cols = jnp.take(keep_all, sources, axis=1)
    wr = wavelet[0, 0]
    wi = wavelet[1, 0]
    gathered = lax.all_to_all(green_freq, "freq", split_axis=2, concat_axis=1, tiled=True)
    both = lax.all_gather(pickcat, "rcv", axis=0, tiled=True)
    dr = data_matrix[0, 0]
    di = data_matrix[1, 0]
    flipped = jnp.concatenate([-both[:, picks:], both[:, :picks]], axis=1)
    multiple = apply_rows(dr, di, both, flipped)
    resid_real = shot_panels[0, 0] - (wr * picked[0] - wi * picked[1] - multiple[:, :picks])
    resid_imag = shot_panels[1, 0] - (wr * picked[1] + wi * picked[0] - multiple[:, picks:])
    residual = jnp.stack([resid_real, resid_imag])[:, None]
    down = ((0,), (0,))
    rboth = jnp.concatenate([resid_real, resid_imag], axis=1)
    rflip = jnp.concatenate([resid_imag, -resid_real], axis=1)
    adjoint = dots(dr, rboth, down) + dots(di, rflip, down)
    local = jnp.concatenate(
        [wr * resid_real + wi * resid_imag, wr * resid_imag - wi * resid_real], axis=1
    )
    direction = local - lax.psum_scatter(adjoint, "rcv", scatter_dimension=0, tiled=True)
    dir_all = lax.all_gather(direction, "rcv", axis=0, tiled=True)
    shrunk = shrink_call(threshold, keep_all, (gathered,))
    back = lax.all_to_all(shrunk, "freq", split_axis=1, concat_axis=2, tiled=True)
    dir_real = direction[:, :picks]
    dir_imag = direction[:, picks:]
    dir_timed = lax.all_to_all(
        jnp.stack([dir_real, dir_imag])[:, None],
        "freq", split_axis=2, concat_axis=1, tiled=True,
    )
    pushed = apply_rows(
        dr, di, dir_all, jnp.concatenate([-dir_all[:, picks:], dir_all[:, :picks]], axis=1)
    )
    image_real = wr * dir_real - wi * dir_imag - pushed[:, :picks]
    image_imag = wr * dir_imag + wi * dir_real - pushed[:, picks:]
    norm_dir = jnp.sum(direction * direction)
    norm_img = jnp.sum(image_real * image_real + image_imag * image_imag)
    totals = lax.psum(jnp.stack([norm_dir, norm_img]), ("freq", "rcv"))
    scalars = jnp.concatenate([threshold, (totals[0] / totals[1])[None]])
    pick_timed = jnp.take(gathered, sources, axis=3)
    cols = shrink_call(scalars, keep_cols, (pick_timed, dir_timed))
    cols_back = lax.all_to_all(cols, "freq", split_axis=1, concat_axis=2, tiled=True)
    cols_back = jnp.concatenate([cols_back[0, 0], cols_back[1, 0]], axis=1)
    hot = sources[:, None] == places[None, :]
    mask = jnp.any(hot, axis=0, keepdims=True).astype(jnp.float32)
    green_next = merge_call(mask, hot.astype(jnp.bfloat16), cols_back, back)
    return (green_next, residual)


def solution(mesh):
    in_specs = (
        P(None, "freq", "rcv", None),
        P(None, "freq", "rcv", None),
        P(None, "freq", "rcv", None),
        P(None, "freq"),
        P(),
        P(),
        P(),
    )
    out_specs = (P(None, "freq", "rcv", None), P(None, "freq", "rcv", None))
    return jax.shard_map(
        on_device, mesh=mesh, in_specs=in_specs, out_specs=out_specs, check_vma=False
    )
```

```python
import functools
import math

import jax
import jax.numpy as jnp
from jax import lax
from jax.experimental import pallas as pl
from jax.experimental.pallas import tpu as pltpu
from jax.sharding import PartitionSpec as P

HIGH = lax.Precision.HIGH
MESH = pl.DeviceIdType.MESH


def transform(points, sign):
    count = len(points)
    if count == 1:
        return points
    if count % 2:
        out = []
        for t in range(count):
            real, imag = points[0]
            for f in range(1, count):
                angle = sign * 2.0 * math.pi * (f * t % count) / count
                c, s = math.cos(angle), math.sin(angle)
                real = real + (c * points[f][0] - s * points[f][1])
                imag = imag + (s * points[f][0] + c * points[f][1])
            out.append((real, imag))
        return out
    even = transform(points[0::2], sign)
    odd = transform(points[1::2], sign)
    low, high = [], []
    for k in range(count // 2):
        er, ei = even[k]
        r, i = odd[k]
        angle = 8 * k / count
        if k == 0:
            tr, ti = r, i
        elif angle == 2:
            tr, ti = (-i, r) if sign > 0 else (i, -r)
        elif angle == 1:
            h = math.sqrt(0.5)
            tr, ti = (h * (r - i), h * (r + i)) if sign > 0 else (h * (r + i), h * (i - r))
        elif angle == 3:
            h = math.sqrt(0.5)
            tr, ti = (-h * (r + i), h * (r - i)) if sign > 0 else (h * (i - r), -h * (r + i))
        else:
            c = math.cos(2 * math.pi * k / count)
            s = sign * math.sin(2 * math.pi * k / count)
            tr, ti = c * r - s * i, s * r + c * i
        low.append((er + tr, ei + ti))
        high.append((er - tr, ei - ti))
    return low + high


def shrink_points(points, keep, level):
    count = len(points)
    timed = transform(points, 1)
    kept = []
    for t, (real, imag) in enumerate(timed):
        size = jnp.sqrt(real * real + imag * imag)
        factor = jnp.maximum(size - level, 0.0) / jnp.maximum(size, level) * keep[t : t + 1]
        factor = factor * (1.0 / count)
        kept.append((factor * real, factor * imag))
    return transform(kept, -1)


def shrink_body(scal_ref, keep_ref, *refs):
    *x_refs, o_ref = refs
    x_ref = x_refs[0]
    count = x_ref.shape[1]
    level = scal_ref[0]

    def lanes(j, carry):
        at = pl.ds(pl.multiple_of(j * 128, 128), 128)
        points = [(x_ref[0, f, :, at], x_ref[1, f, :, at]) for f in range(count)]
        if len(x_refs) == 2:
            d_ref = x_refs[1]
            step = scal_ref[1]
            points = [
                (r + step * d_ref[0, f, :, at], i + step * d_ref[1, f, :, at])
                for f, (r, i) in enumerate(points)
            ]
        out = shrink_points(points, keep_ref[:, at], level)
        for f in range(count):
            o_ref[0, f, :, at] = out[f][0]
            o_ref[1, f, :, at] = out[f][1]
        return carry

    lax.fori_loop(0, x_ref.shape[3] // 128, lanes, 0)


def shrink_call(scalars, keep, arrays):
    two, count, rows, width = arrays[0].shape
    tile = 8 if rows % 8 == 0 else rows
    if rows % 24 == 0 and width <= 512:
        tile = 24
    block = pl.BlockSpec((two, count, tile, width), lambda j: (0, 0, j, 0))
    size = arrays[0].size * 4
    return pl.pallas_call(
        shrink_body,
        grid=(rows // tile,),
        in_specs=[
            pl.BlockSpec(memory_space=pltpu.SMEM),
            pl.BlockSpec((count, width), lambda j: (0, 0)),
        ]
        + [block] * len(arrays),
        out_specs=block,
        out_shape=jax.ShapeDtypeStruct(arrays[0].shape, jnp.float32),
        cost_estimate=pl.CostEstimate(
            flops=40 * arrays[0].size, bytes_accessed=size * (1 + len(arrays)), transcendentals=0
        ),
    )(scalars, keep, *arrays)


def merge_body(mask_ref, hot_ref, cols_ref, back_ref, o_ref):
    hot = hot_ref[...]
    mask = mask_ref[...] > 0.5
    for part in range(2):
        x = cols_ref[:, part * hot.shape[0] : (part + 1) * hot.shape[0]]
        hi = x.astype(jnp.bfloat16)
        rest = x - hi.astype(jnp.float32)
        mid = rest.astype(jnp.bfloat16)
        low = (rest - mid.astype(jnp.float32)).astype(jnp.bfloat16)
        spread = (
            jnp.dot(hi, hot, preferred_element_type=jnp.float32)
            + jnp.dot(mid, hot, preferred_element_type=jnp.float32)
        ) + jnp.dot(low, hot, preferred_element_type=jnp.float32)
        o_ref[part, 0] = jnp.where(mask, spread, back_ref[part, 0])


def merge_call(mask, hot, cols, back):
    two, one, rows, width = back.shape
    picked = hot.shape[0]
    tile = rows // 4 if rows % 32 == 0 else rows
    return pl.pallas_call(
        merge_body,
        grid=(rows // tile,),
        in_specs=[
            pl.BlockSpec((1, width), lambda i: (0, 0)),
            pl.BlockSpec((picked, width), lambda i: (0, 0)),
            pl.BlockSpec((tile, two * picked), lambda i: (i, 0)),
            pl.BlockSpec((two, one, tile, width), lambda i: (0, 0, i, 0)),
        ],
        out_specs=pl.BlockSpec((two, one, tile, width), lambda i: (0, 0, i, 0)),
        out_shape=jax.ShapeDtypeStruct(back.shape, jnp.float32),
    )(mask, hot, cols, back)


def dots(lhs, rhs, contract):
    return lax.dot_general(lhs, rhs, (contract, ((), ())), precision=HIGH)


def apply_rows(data_real, data_imag, both, flipped):
    ahead = (((1,), (0,)))
    return dots(data_real, both, ahead) + dots(data_imag, flipped, ahead)


ANY = pl.BlockSpec(memory_space=pltpu.HBM)
VMEM = pl.BlockSpec(memory_space=pltpu.VMEM)
DMA = pltpu.SemaphoreType.DMA


SMEM = pl.BlockSpec(memory_space=pltpu.SMEM)


def halves(x):
    hi = x.astype(jnp.bfloat16)
    return hi, (x - hi.astype(jnp.float32)).astype(jnp.bfloat16)


def thirds(x):
    hi, mid = halves(x)
    rest = x - hi.astype(jnp.float32) - mid.astype(jnp.float32)
    return jnp.concatenate([hi, mid, rest.astype(jnp.bfloat16)], axis=0)


def select(x, hot):
    rows = x.shape[0]
    out = jnp.dot(thirds(x), hot, preferred_element_type=jnp.float32)
    return (out[:rows] + out[rows : 2 * rows]) + out[2 * rows :]


def spread(x, hot):
    hi, mid = halves(x)
    low = (x - hi.astype(jnp.float32) - mid.astype(jnp.float32)).astype(jnp.bfloat16)
    return (
        jnp.dot(hi, hot, preferred_element_type=jnp.float32)
        + jnp.dot(mid, hot, preferred_element_type=jnp.float32)
    ) + jnp.dot(low, hot, preferred_element_type=jnp.float32)


def six(parts, contract):
    total = None
    for (lh, ll), (rh, rl) in parts:
        for x, y in ((lh, rl), (ll, rh), (lh, rh)):
            term = lax.dot_general(
                x, y, (contract, ((), ())), preferred_element_type=jnp.float32
            )
            total = term if total is None else total + term
    return total


def piece_of(width):
    for piece in (768, 512, 256):
        if width % piece == 0:
            return piece
    return width


def apply_data(data, x_ref, acc):
    half = x_ref.shape[1] // 2
    piece = piece_of(x_ref.shape[0])
    acc[...] = jnp.zeros_like(acc)

    def chunk(i, carry):
        at = pl.ds(pl.multiple_of(i * piece, piece), piece)
        x = x_ref[at, :]
        turned = jnp.concatenate([-x[:, half:], x[:, :half]], axis=1)
        acc[...] += six(
            [
                ((data[0, 0, :, at], data[0, 1, :, at]), halves(x)),
                ((data[1, 0, :, at], data[1, 1, :, at]), halves(turned)),
            ],
            ((1,), (0,)),
        )
        return carry

    lax.fori_loop(0, x_ref.shape[0] // piece, chunk, 0)


def apply_adjoint(data, x, out):
    half = x.shape[1] // 2
    piece = piece_of(out.shape[0])
    straight = halves(x)
    turned = halves(jnp.concatenate([x[:, half:], -x[:, :half]], axis=1))

    def chunk(i, carry):
        at = pl.ds(pl.multiple_of(i * piece, piece), piece)
        out[at, :] = six(
            [
                ((data[0, 0, :, at], data[0, 1, :, at]), straight),
                ((data[1, 0, :, at], data[1, 1, :, at]), turned),
            ],
            ((0,), (0,)),
        )
        return carry

    lax.fori_loop(0, out.shape[0] // piece, chunk, 0)


class Gather:
    def __init__(self, size, buf, sends, recvs):
        self.size, self.buf, self.sends, self.recvs = size, buf, sends, recvs
        self.z = lax.axis_index("rcv")

    def ways(self, step):
        z, last = self.z, self.size - 1
        rows = self.buf.shape[0] // self.size
        for way in range(2):
            if way == 0:
                block, to = jnp.maximum(z - step, 0), jnp.minimum(z + 1, last)
                sent = (z < last) & (z >= step)
                got = z >= step + 1
            else:
                block, to = jnp.minimum(z + step, last), jnp.maximum(z - 1, 0)
                sent = (z > 0) & (z + step <= last)
                got = z + 1 + step <= last
            part = self.buf.at[pl.ds(pl.multiple_of(block * rows, 8), rows), :]
            copy = pltpu.make_async_remote_copy(
                part, part, self.sends.at[way, step], self.recvs.at[way, step],
                device_id={"rcv": to}, device_id_type=MESH,
            )
            yield copy, sent, got

    def start(self, step):
        for copy, sent, _ in self.ways(step):
            pl.when(sent)(copy.start)

    def recv(self, step):
        for copy, _, got in self.ways(step):
            pl.when(got)(copy.wait_recv)

    def drain(self):
        for step in range(self.size - 1):
            for copy, sent, _ in self.ways(step):
                pl.when(sent)(copy.wait_send)


class Scatter:
    def __init__(self, size, terms, held, sends, recvs):
        self.size, self.terms, self.held = size, terms, held
        self.sends, self.recvs = sends, recvs
        self.z = lax.axis_index("rcv")

    def ways(self, step):
        z, last = self.z, self.size - 1
        rows = self.terms.shape[0] // self.size
        for way in range(2):
            if way == 0:
                far, to = z, jnp.minimum(z + 1, last)
                block = jnp.minimum(last - step + z, last)
                more, less = z < last, z > 0
            else:
                far, to = last - z, jnp.maximum(z - 1, 0)
                block = jnp.maximum(step - last + z, 0)
                more, less = z > 0, z < last
            own = self.terms.at[pl.ds(pl.multiple_of(block * rows, 8), rows), :]
            got = less & (step >= far - 1)
            yield way, own, to, more & (far == 0), more & (far > 0) & (step >= far), got

    def copy(self, src, way, step, to):
        return pltpu.make_async_remote_copy(
            src, self.held.at[way, step], self.sends.at[way, step], self.recvs.at[way, step],
            device_id={"rcv": to}, device_id_type=MESH,
        )

    def start(self, step):
        for way, own, to, first, later, _ in self.ways(step):
            pl.when(first)(self.copy(own, way, step, to).start)
            if step:
                self.pass_on(way, own, to, step, later)

    def pass_on(self, way, own, to, step, later):
        @pl.when(later)
        def _():
            self.held[way, step - 1] = self.held[way, step - 1] + own[...]
            self.copy(self.held.at[way, step - 1], way, step, to).start()

    def recv(self, step):
        for way, own, to, _, _, got in self.ways(step):
            pl.when(got)(self.copy(own, way, step, to).wait_recv)

    def drain(self):
        for step in range(self.size - 1):
            for way, own, to, first, later, _ in self.ways(step):
                pl.when(first | later)(self.copy(own, way, step, to).wait_send)


def greet(freqs, size):
    me = lax.axis_index("freq")
    z = lax.axis_index("rcv")
    barrier = pltpu.get_barrier_semaphore()
    for k in range(1, freqs):
        pl.semaphore_signal(
            barrier, inc=1, device_id={"freq": (me + k) % freqs}, device_id_type=MESH
        )
    for k in range(1, size):
        pl.semaphore_signal(barrier, inc=1, device_id={"rcv": (z + k) % size}, device_id_type=MESH)
    pl.semaphore_wait(barrier, freqs + size - 2)


LINE = 8


def rows_at(at, count):
    return pl.ds(pl.multiple_of(at, 8), count)


def main_body(
    freqs, size, level_ref, wave, srcs, support, green, data_hbm, shots_hbm,
    gathered, shrunk, back, tails, cols_out, resid_hbm, hot_hbm, mask_hbm,
    residual, hot_out, mask_out,
    big, data, whole, dir_all, adjoint, held, local, shots, image, hot, fill, lead,
    keep, keep_cols, timed, cols, norms, freq_box, rcv_box,
    gload, sload, load, put, fsend, frecv, fown, bsend, brecv, bown,
    zsend, zrecv, dsend, drecv, down, csend, crecv, cown, nfs, nfr, nzs, nzr,
):
    me = lax.axis_index("freq")
    z = lax.axis_index("rcv")
    _, _, rows, width = green.shape
    deep = rows // freqs
    lines = deep // LINE
    picks = srcs.shape[1]
    half = picks // 2
    head = width - picks
    mine = rows_at(z * rows, rows)
    parts = gload.shape[0]
    tall = rows // parts

    def loading(j):
        at = rows_at(j * tall, tall)
        return pltpu.make_async_copy(green.at[:, 0, at, :], big.at[:, at, :], gload.at[j])

    for j in range(parts):
        loading(j).start()
    fetch_shots = pltpu.make_async_copy(shots_hbm.at[:, 0], shots, sload)
    fetch_shots.start()
    slots = [box.at[c, rows_at(n * rows, rows), :]
             for box in (adjoint, dir_all) for c in range(2) for n in range(size)]
    slots += [held.at[c, way, n] for c in range(2) for way in range(2) for n in range(size - 1)]
    places = [(part, at) for part in range(2) for at in range(0, width, picks)]
    slots = slots[: len(places)]

    def fetching(n):
        part, at = places[n]
        return pltpu.make_async_copy(
            data_hbm.at[part, 0, :, pl.ds(at, picks)], slots[n], load.at[n]
        )

    for n in range(len(places)):
        fetching(n).start()

    def packed(i, to):
        if isinstance(i, int) and i == 0:
            return lead.at[:, rows_at(to * LINE, LINE), :]
        return big.at[:, rows_at(to * deep + i * LINE, LINE), pl.ds(0, head)]

    def forth(i, k):
        to = (me + k) % freqs
        return pltpu.make_async_remote_copy(
            packed(i, to), gathered.at[:, me, rows_at(i * LINE, LINE), :],
            fsend.at[i, k], frecv.at[i, k],
            device_id={"freq": to}, device_id_type=MESH,
        )

    def forth_own(i):
        return pltpu.make_async_copy(
            packed(i, me), gathered.at[:, me, rows_at(i * LINE, LINE), :], fown.at[i]
        )

    def send_forth(i):
        for k in range(1, freqs):
            forth(i, k).start()
        forth_own(i).start()

    place = lax.broadcasted_iota(jnp.int32, (width, picks), 0)
    hot[...] = jnp.where(place == srcs[...], 1.0, 0.0).astype(jnp.bfloat16)
    before = jnp.where(srcs[...] < place, 1.0, 0.0)
    ones = jnp.ones((8, picks), jnp.bfloat16)
    across_lanes = (((1,), (1,)), ((), ()))
    mask_out[...] = lax.dot_general(
        ones, hot[...], across_lanes, preferred_element_type=jnp.float32
    )
    rank = lax.dot_general(
        ones, before.astype(jnp.bfloat16), across_lanes, preferred_element_type=jnp.float32
    )
    ends = jnp.sum(before[head:, :], axis=1, keepdims=True)
    spare = 1.0 - jnp.sum(
        hot[head:, :].astype(jnp.float32), axis=1, keepdims=True
    )
    order = lax.broadcasted_iota(jnp.int32, (picks, 1), 0).astype(jnp.float32)
    order = order - (ends - ends[0:1, :])
    taken = mask_out[0:1, :head] > 0.5
    fill[...] = jnp.where(
        taken & (spare > 0.5) & (rank[0:1, :head] == order), 1.0, 0.0
    ).astype(jnp.bfloat16)

    def pack(x):
        got = spread(x[:, head:], fill[...])
        return jnp.where(mask_out[0:1, :head] > 0.5, got, x[:, :head])

    def line_of(i):
        return jnp.concatenate(
            [big[part, rows_at(o * deep + i * LINE, LINE), :] for part in range(2)
             for o in range(freqs)], axis=0,
        )

    for j in range(parts):
        loading(j).wait()
    lead_rows = pack(line_of(0))
    for part in range(2):
        lead[part] = lead_rows[part * freqs * LINE : (part + 1) * freqs * LINE]
    keep_all = support[...].astype(jnp.float32)
    keep[...] = jnp.where(
        taken,
        jnp.dot(
            keep_all[:, head:].astype(jnp.bfloat16), fill[...], preferred_element_type=jnp.float32
        ),
        keep_all[:, :head],
    )
    keep_cols[...] = jnp.dot(
        keep_all.astype(jnp.bfloat16), hot[...], preferred_element_type=jnp.float32
    )
    greet(freqs, size)
    send_forth(0)

    def pick(j, carry):
        at = rows_at(j * tall, tall)
        for part in range(2):
            out = select(big[part, at, :], hot[...])
            to = rows_at(z * rows + j * tall, tall)
            for c in range(2):
                whole[c, to, part * half : (part + 1) * half] = out[:, c * half : (c + 1) * half]
        return carry

    lax.fori_loop(0, parts, pick, 0)
    for n, (part, at) in enumerate(places):
        fetching(n).wait()
        for row in range(0, rows, rows // 2):
            there = slice(row, row + rows // 2)
            hi, lo = halves(slots[n][there, :])
            data[part, 0, there, at : at + picks] = hi
            data[part, 1, there, at : at + picks] = lo

    first = [Gather(size, whole.at[c], zsend.at[c], zrecv.at[c]) for c in range(2)]
    second = [Gather(size, dir_all.at[c], zsend.at[2 + c], zrecv.at[2 + c]) for c in range(2)]
    sums = [
        Scatter(size, adjoint.at[c], held.at[c], zsend.at[4 + c], zrecv.at[4 + c])
        for c in range(2)
    ]
    last = size - 2
    first[0].start(0)
    def pack_line(i, carry):
        done = pack(line_of(i))
        for part in range(2):
            for o in range(freqs):
                row = (part * freqs + o) * LINE
                big[part, rows_at(o * deep + i * LINE, LINE), 0:head] = done[row : row + LINE]
        return carry

    lax.fori_loop(1, lines, pack_line, 0)
    for i in range(1, lines):
        send_forth(i)
    for at in range(0, width, picks):
        hot_out[:, at : at + picks] = hot[at : at + picks, :].astype(jnp.float32).T.astype(
            jnp.bfloat16
        )

    def shrink(lo, count):
        for i in range(lo, lo + count):
            for k in range(1, freqs):
                forth(i, k).wait_recv()
            forth_own(i).wait()
        block = pl.BlockSpec((2, freqs, LINE, head), lambda j: (0, 0, lo + j, 0))
        pltpu.emit_pipeline(
            lambda x, o: shrink_body(level_ref, keep, x, o),
            grid=(count,), in_specs=[block], out_specs=[block],
        )(gathered, shrunk)

    def back_ends(i, to):
        line = min(i, lines - 1)
        part = slice(0, 2) if i < lines - 1 else slice(i - line, i - line + 1)
        return (
            shrunk.at[part, to, pl.ds(line * LINE, LINE), :],
            back.at[part, 0, rows_at(me * deep + line * LINE, LINE), :],
        )

    def back_copy(i, k):
        to = (me + k) % freqs
        return pltpu.make_async_remote_copy(
            *back_ends(i, to), bsend.at[i, k], brecv.at[i, k],
            device_id={"freq": to}, device_id_type=MESH,
        )

    def back_own(i):
        return pltpu.make_async_copy(*back_ends(i, me), bown.at[i])

    def give(lo, count):
        for i in range(lo, lo + count):
            for k in range(1, freqs):
                back_copy(i, k).start()
            back_own(i).start()

    def rows_copy(c, k):
        to = (me + k) % freqs
        return pltpu.make_async_remote_copy(
            local.at[c, rows_at(to * deep, deep), :], timed.at[c, me],
            dsend.at[c, k], drecv.at[c, k],
            device_id={"freq": to}, device_id_type=MESH,
        )

    def rows_own(c):
        return pltpu.make_async_copy(
            local.at[c, rows_at(me * deep, deep), :], timed.at[c, me], down.at[c]
        )

    wr, wi = wave[0], wave[1]
    re, im = slice(0, half), slice(half, 2 * half)

    def residual_of(c):
        apply_data(data, whole.at[c], image)
        at = slice(c * half, (c + 1) * half)
        pr, pi = whole[c, mine, re], whole[c, mine, im]
        rr = shots[0, :, at] - (wr * pr - wi * pi - image[:, re])
        ri = shots[1, :, at] - (wr * pi + wi * pr - image[:, im])
        residual[0, 0, :, at] = rr
        residual[1, 0, :, at] = ri
        local[c, :, re] = wr * rr + wi * ri
        local[c, :, im] = wr * ri - wi * rr
        apply_adjoint(data, jnp.concatenate([rr, ri], axis=1), adjoint.at[c])

    def direction_of(c):
        dir_all[c, mine, :] = local[c] - adjoint[c, mine, :]

        @pl.when(z > 0)
        def _():
            dir_all[c, mine, :] = dir_all[c, mine, :] - held[c, 0, last]

        @pl.when(z < size - 1)
        def _():
            dir_all[c, mine, :] = dir_all[c, mine, :] - held[c, 1, last]

    def send_update(c, step):
        local[c] = whole[c, mine, :] + step * dir_all[c, mine, :]
        for k in range(1, freqs):
            rows_copy(c, k).start()
        rows_own(c).start()

    def image_of(c):
        apply_data(data, dir_all.at[c], image)
        dr, di = dir_all[c, mine, re], dir_all[c, mine, im]
        gr = wr * dr - wi * di - image[:, re]
        gi = wr * di + wi * dr - image[:, im]
        return jnp.sum(dr * dr + di * di), jnp.sum(gr * gr + gi * gi)

    first[0].recv(0)
    first[0].start(1)
    fetch_shots.wait()
    first[0].recv(1)
    first[0].start(2)
    first[1].start(0)
    shrink(0, 2)
    first[0].recv(2)
    residual_of(0)
    sums[0].start(0)
    first[1].recv(0)
    first[1].start(1)
    shrink(2, 2)
    give(0, 4)
    sums[0].recv(0)
    sums[0].start(1)
    first[1].recv(1)
    first[1].start(2)
    shrink(4, 1)
    give(4, 1)
    sums[0].recv(1)
    sums[0].start(2)
    first[1].recv(2)
    residual_of(1)
    sums[1].start(0)
    puts = [
        pltpu.make_async_copy(src, dst, put.at[n])
        for n, (src, dst) in enumerate(
            ((residual, resid_hbm), (hot_out, hot_hbm), (mask_out, mask_hbm))
        )
    ]
    for copy in puts:
        copy.start()
    sums[0].recv(2)
    direction_of(0)
    second[0].start(0)
    shrink(5, 2)
    give(5, 2)
    sums[1].recv(0)
    sums[1].start(1)
    second[0].recv(0)
    second[0].start(1)
    shrink(7, 1)
    give(7, 1)
    sums[1].recv(1)
    sums[1].start(2)
    second[0].recv(1)
    second[0].start(2)
    shrink(8, lines - 8)
    give(8, lines - 8)
    sums[1].recv(2)
    direction_of(1)
    second[1].start(0)
    second[0].recv(2)
    first_norms = image_of(0)
    second[1].recv(0)
    second[1].start(1)
    second[1].recv(1)
    second[1].start(2)
    second[1].recv(2)
    second_norms = image_of(1)

    for n in range(2):
        norms[n] = jnp.full((8, 128), first_norms[n] + second_norms[n])

    def along(k):
        return pltpu.make_async_remote_copy(
            freq_box.at[0], freq_box.at[k], nfs.at[k], nfr.at[k],
            device_id={"freq": (me + k) % freqs}, device_id_type=MESH,
        )

    def across(k):
        return pltpu.make_async_remote_copy(
            norms, rcv_box.at[k], nzs.at[k], nzr.at[k],
            device_id={"rcv": (z + k) % size}, device_id_type=MESH,
        )

    for k in range(1, size):
        across(k).start()
    line_sum = norms[...]
    for k in range(1, size):
        across(k).wait_recv()
        line_sum = line_sum + rcv_box[k]
    freq_box[0] = line_sum
    for k in range(1, freqs):
        along(k).start()
    give(lines, 1)
    total = line_sum
    for k in range(1, freqs):
        along(k).wait_recv()
        total = total + freq_box[k]
    step = total[0] / total[1]
    level = level_ref[0]
    for c in range(2):
        send_update(c, step[0:1, 0:1])

    def cols_copy(c, k):
        to = (me + k) % freqs
        return pltpu.make_async_remote_copy(
            cols.at[c, to], cols_out.at[rows_at(me * deep, deep), pl.ds(c * picks, picks)],
            csend.at[c, k], crecv.at[c, k],
            device_id={"freq": to}, device_id_type=MESH,
        )

    def cols_own(c):
        return pltpu.make_async_copy(
            cols.at[c, me], cols_out.at[rows_at(me * deep, deep), pl.ds(c * picks, picks)],
            cown.at[c],
        )

    for c in range(2):
        for k in range(1, freqs):
            rows_copy(c, k).wait_recv()
        rows_own(c).wait()

        def tile(i, carry):
            at = rows_at(i * 8, 8)
            for lane in range(0, half, 128):
                points = [
                    (timed[c, f, at, lane : lane + 128],
                     timed[c, f, at, half + lane : half + lane + 128])
                    for f in range(freqs)
                ]
                good = keep_cols[:, c * half + lane : c * half + lane + 128]
                done = shrink_points(points, good, level)
                for f in range(freqs):
                    cols[c, f, at, lane : lane + 128] = done[f][0]
                    cols[c, f, at, half + lane : half + lane + 128] = done[f][1]
            return carry

        lax.fori_loop(0, deep // 8, tile, 0)
        for k in range(1, freqs):
            cols_copy(c, k).start()
        cols_own(c).start()
    for i in range(lines + 1):
        for k in range(1, freqs):
            back_copy(i, k).wait()
        back_own(i).wait()

    def tail(x_ref, o_ref):
        x = jnp.concatenate([x_ref[0, 0], x_ref[1, 0]], axis=0)
        n = x.shape[0]
        out = lax.dot_general(
            thirds(x), fill[...], across_lanes, preferred_element_type=jnp.float32
        )
        out = (out[:n] + out[n : 2 * n]) + out[2 * n :]
        o_ref[0, 0] = out[: n // 2]
        o_ref[1, 0] = out[n // 2 :]

    pltpu.emit_pipeline(
        tail, grid=(rows // deep,),
        in_specs=[pl.BlockSpec((2, 1, deep, head), lambda j: (0, 0, j, 0))],
        out_specs=[pl.BlockSpec((2, 1, deep, picks), lambda j: (0, 0, j, 0))],
    )(back, tails)
    for copy in puts:
        copy.wait()
    for group in first + second + sums:
        group.drain()
    for i in range(lines):
        for k in range(1, freqs):
            forth(i, k).wait_send()
    for k in range(1, freqs):
        along(k).wait_send()
        for c in range(2):
            rows_copy(c, k).wait_send()
            cols_copy(c, k).wait()
    for c in range(2):
        cols_own(c).wait()
    for k in range(1, size):
        across(k).wait_send()


def main_call(freqs, size, level, wave, srcs, support, green, data, shots):
    two, _, rows, width = green.shape
    picks = srcs.shape[1]
    deep = rows // freqs
    lines = deep // LINE
    f32, bf16 = jnp.float32, jnp.bfloat16
    split = jax.ShapeDtypeStruct((two, freqs, deep, width - picks), f32)
    vmem = pltpu.VMEM
    return pl.pallas_call(
        functools.partial(main_body, freqs, size),
        out_shape=(
            split,
            split,
            jax.ShapeDtypeStruct((two, 1, rows, width - picks), f32),
            jax.ShapeDtypeStruct((two, 1, rows, picks), f32),
            jax.ShapeDtypeStruct((rows, two * picks), f32),
            jax.ShapeDtypeStruct((two, 1, rows, picks), f32),
            jax.ShapeDtypeStruct((picks, width), bf16),
            jax.ShapeDtypeStruct((8, width), f32),
        ),
        in_specs=[SMEM, SMEM, VMEM, VMEM, ANY, ANY, ANY],
        out_specs=(ANY,) * 8,
        scratch_shapes=[
            vmem((two, 1, rows, picks), f32),
            vmem((picks, width), bf16),
            vmem((8, width), f32),
            vmem((two, rows, width), f32),
            vmem((two, 2, rows, width), bf16),
            vmem((2, size * rows, picks), f32),
            vmem((2, size * rows, picks), f32),
            vmem((2, size * rows, picks), f32),
            vmem((2, 2, size - 1, rows, picks), f32),
            vmem((2, rows, picks), f32),
            vmem((two, rows, picks), f32),
            vmem((rows, picks), f32),
            vmem((width, picks), bf16),
            vmem((picks, width - picks), bf16),
            vmem((two, freqs * LINE, width - picks), f32),
            vmem((8, width - picks), f32),
            vmem((8, picks), f32),
            vmem((2, freqs, deep, picks), f32),
            vmem((2, freqs, deep, picks), f32),
            vmem((2, 8, 128), f32),
            vmem((freqs, 2, 8, 128), f32),
            vmem((size, 2, 8, 128), f32),
            DMA((4,)), DMA(()), DMA((2 * (width // picks),)), DMA((3,)),
            DMA((lines, freqs)), DMA((lines, freqs)), DMA((lines,)),
            DMA((lines + 1, freqs)), DMA((lines + 1, freqs)), DMA((lines + 1,)),
            DMA((6, 2, size)), DMA((6, 2, size)),
            DMA((2, freqs)), DMA((2, freqs)), DMA((2,)),
            DMA((2, freqs)), DMA((2, freqs)), DMA((2,)),
            DMA((freqs,)), DMA((freqs,)), DMA((size,)), DMA((size,)),
        ],
        compiler_params=pltpu.CompilerParams(
            collective_id=0, has_side_effects=True, vmem_limit_bytes=67043328
        ),
    )(level, wave, srcs, support, green, data, shots)


def join_body(mask_ref, hot_ref, cols_ref, back_ref, tail_ref, resid_ref, o_ref, r_ref, stacked):
    picks = hot_ref.shape[0]
    half = picks // 2
    rows = cols_ref.shape[0]
    mask = mask_ref[0:1, :] > 0.5

    @pl.when(pl.program_id(0) == 0)
    def _():
        for n in range(3):
            stacked[n * picks : (n + 1) * picks, :] = hot_ref[...]

    both = [
        jnp.concatenate(
            [cols_ref[:, at : at + half], cols_ref[:, picks + at : picks + at + half]], axis=1
        )
        for at in (0, half)
    ]
    x = jnp.concatenate(both, axis=0)
    hi, mid = halves(x)
    low = (x - hi.astype(jnp.float32) - mid.astype(jnp.float32)).astype(jnp.bfloat16)
    wide = jnp.dot(
        jnp.concatenate([hi, mid, low], axis=1), stacked[...], preferred_element_type=jnp.float32
    )
    for part in range(2):
        new = wide[part * rows : (part + 1) * rows]
        head = back_ref.shape[3]
        o_ref[part, 0, :, :head] = jnp.where(mask[:, :head], new[:, :head], back_ref[part, 0])
        o_ref[part, 0, :, head:] = jnp.where(mask[:, head:], new[:, head:], tail_ref[part, 0])
    r_ref[...] = resid_ref[...]


def join_call(mask, hot, cols, back, tails, resid):
    two, one, rows, head = back.shape
    picks, width = hot.shape
    tile = rows // 6 if rows % 48 == 0 else rows
    wide = pl.BlockSpec((two, one, tile, width), lambda i: (0, 0, i, 0))
    thin = pl.BlockSpec((two, one, tile, picks), lambda i: (0, 0, i, 0))
    return pl.pallas_call(
        join_body,
        grid=(rows // tile,),
        in_specs=[
            pl.BlockSpec((8, width), lambda i: (0, 0)),
            pl.BlockSpec((picks, width), lambda i: (0, 0)),
            pl.BlockSpec((tile, two * picks), lambda i: (i, 0)),
            pl.BlockSpec((two, one, tile, head), lambda i: (0, 0, i, 0)),
            thin,
            thin,
        ],
        out_specs=[wide, thin],
        out_shape=[
            jax.ShapeDtypeStruct((two, one, rows, width), jnp.float32),
            jax.ShapeDtypeStruct(resid.shape, jnp.float32),
        ],
        scratch_shapes=[pltpu.VMEM((3 * picks, width), jnp.bfloat16)],
    )(mask, hot, cols, back, tails, resid)


def pick_body(hot_ref, x_ref, o_ref):
    picks = hot_ref.shape[1]
    hot = hot_ref[...]
    for part in range(2):
        x = x_ref[part, 0]
        hi = x.astype(jnp.bfloat16)
        rest = x - hi.astype(jnp.float32)
        mid = rest.astype(jnp.bfloat16)
        low = (rest - mid.astype(jnp.float32)).astype(jnp.bfloat16)
        o_ref[:, part * picks : (part + 1) * picks] = (
            jnp.dot(hi, hot, preferred_element_type=jnp.float32)
            + jnp.dot(mid, hot, preferred_element_type=jnp.float32)
        ) + jnp.dot(low, hot, preferred_element_type=jnp.float32)


def pick_call(hot, green):
    two, one, rows, width = green.shape
    picks = hot.shape[1]
    tile = rows // 4 if rows % 32 == 0 else rows
    return pl.pallas_call(
        pick_body,
        grid=(rows // tile,),
        in_specs=[
            pl.BlockSpec((width, picks), lambda i: (0, 0)),
            pl.BlockSpec((two, one, tile, width), lambda i: (0, 0, i, 0)),
        ],
        out_specs=pl.BlockSpec((tile, 2 * picks), lambda i: (i, 0)),
        out_shape=jax.ShapeDtypeStruct((rows, 2 * picks), jnp.float32),
    )(hot, green)


def on_device(green_freq, data_matrix, shot_panels, wavelet, sources, support, threshold):
    width = green_freq.shape[3]
    rows_here = green_freq.shape[2]
    picks = sources.shape[0]
    freqs = lax.axis_size("freq")
    size = lax.axis_size("rcv")
    fast = rows_here % (LINE * freqs) == 0 and size > 2 and rows_here // freqs >= 9 * LINE
    fast = fast and rows_here % 32 == 0 and width % picks == 0 and picks % 256 == 0
    fast = fast and 2 * (width // picks) <= 8 * size - 4
    if fast:
        _, _, back, tails, cols, resid, hot, mask = main_call(
            freqs, size, threshold, wavelet[:, 0], sources[None, :], support,
            green_freq, data_matrix, shot_panels,
        )
        green_next, residual = join_call(mask, hot, cols, back, tails, resid)
        return (green_next, residual)
    keep_all = support.astype(jnp.float32)
    places = jnp.arange(width, dtype=jnp.int32)
    pickcat = pick_call((places[:, None] == sources[None, :]).astype(jnp.bfloat16), green_freq)
    picked = (pickcat[:, :picks], pickcat[:, picks:])
    keep_cols = jnp.take(keep_all, sources, axis=1)
    wr = wavelet[0, 0]
    wi = wavelet[1, 0]
    gathered = lax.all_to_all(green_freq, "freq", split_axis=2, concat_axis=1, tiled=True)
    both = lax.all_gather(pickcat, "rcv", axis=0, tiled=True)
    dr = data_matrix[0, 0]
    di = data_matrix[1, 0]
    flipped = jnp.concatenate([-both[:, picks:], both[:, :picks]], axis=1)
    multiple = apply_rows(dr, di, both, flipped)
    resid_real = shot_panels[0, 0] - (wr * picked[0] - wi * picked[1] - multiple[:, :picks])
    resid_imag = shot_panels[1, 0] - (wr * picked[1] + wi * picked[0] - multiple[:, picks:])
    residual = jnp.stack([resid_real, resid_imag])[:, None]
    down = ((0,), (0,))
    rboth = jnp.concatenate([resid_real, resid_imag], axis=1)
    rflip = jnp.concatenate([resid_imag, -resid_real], axis=1)
    adjoint = dots(dr, rboth, down) + dots(di, rflip, down)
    local = jnp.concatenate(
        [wr * resid_real + wi * resid_imag, wr * resid_imag - wi * resid_real], axis=1
    )
    direction = local - lax.psum_scatter(adjoint, "rcv", scatter_dimension=0, tiled=True)
    dir_all = lax.all_gather(direction, "rcv", axis=0, tiled=True)
    shrunk = shrink_call(threshold, keep_all, (gathered,))
    back = lax.all_to_all(shrunk, "freq", split_axis=1, concat_axis=2, tiled=True)
    dir_real = direction[:, :picks]
    dir_imag = direction[:, picks:]
    dir_timed = lax.all_to_all(
        jnp.stack([dir_real, dir_imag])[:, None],
        "freq", split_axis=2, concat_axis=1, tiled=True,
    )
    pushed = apply_rows(
        dr, di, dir_all, jnp.concatenate([-dir_all[:, picks:], dir_all[:, :picks]], axis=1)
    )
    image_real = wr * dir_real - wi * dir_imag - pushed[:, :picks]
    image_imag = wr * dir_imag + wi * dir_real - pushed[:, picks:]
    norm_dir = jnp.sum(direction * direction)
    norm_img = jnp.sum(image_real * image_real + image_imag * image_imag)
    totals = lax.psum(jnp.stack([norm_dir, norm_img]), ("freq", "rcv"))
    scalars = jnp.concatenate([threshold, (totals[0] / totals[1])[None]])
    pick_timed = jnp.take(gathered, sources, axis=3)
    cols = shrink_call(scalars, keep_cols, (pick_timed, dir_timed))
    cols_back = lax.all_to_all(cols, "freq", split_axis=1, concat_axis=2, tiled=True)
    cols_back = jnp.concatenate([cols_back[0, 0], cols_back[1, 0]], axis=1)
    hot = sources[:, None] == places[None, :]
    mask = jnp.any(hot, axis=0, keepdims=True).astype(jnp.float32)
    green_next = merge_call(mask, hot.astype(jnp.bfloat16), cols_back, back)
    return (green_next, residual)


def solution(mesh):
    in_specs = (
        P(None, "freq", "rcv", None),
        P(None, "freq", "rcv", None),
        P(None, "freq", "rcv", None),
        P(None, "freq"),
        P(),
        P(),
        P(),
    )
    out_specs = (P(None, "freq", "rcv", None), P(None, "freq", "rcv", None))
    return jax.shard_map(
        on_device, mesh=mesh, in_specs=in_specs, out_specs=out_specs, check_vma=False
    )
```
